512 devices in a mesh: lon: 32 (over z_lo, y), lat: 16 (over z_hi, x, core).
Axes of the slice: x: 4, y: 8, z: 8 (z_hi: 2, z_lo: 4; z = z_hi * 4 + z_lo), core: 2. Of those that a mesh axis runs over, the one named last changes fastest.
Arguments:
- wind_u: float32 [720, 1440, 16], P('lat', 'lon'), may hold values from -6 to 6
- wind_v: float32 [720, 1440, 16], P('lat', 'lon'), may hold values from -6 to 6
- vorticity: float32 [720, 1440, 16], P('lat', 'lon'), may hold values from -6 to 6
- sample_level: int32 [16], replicated, may hold values from 0 to 1, as said below
- slot_wavenumber: int32 [736], P('lon'), may hold values from -1 to 719, as said below
- legendre_p: bfloat16 [720, 529920], P('lat', 'lon'), may hold values from -5 to 5
- legendre_h: bfloat16 [720, 529920], P('lat', 'lon'), may hold values from -5 to 5
Outputs:
- spectra: float32 [2, 529920], P(None, ('lon', 'lat'))
The draws below stay inside these ranges and needn't reach their ends.
Inputs may be any that keep to these rules, and one draw needn't show every extreme that they name: `sample_level`: each level is named by exactly 8 samples. `slot_wavenumber`: each wavenumber from 0 to 719 stands in exactly one slot; the remaining slots hold -1.
All inputs are finite; a program needn't handle non-finite values.
Results may differ from the reference program's by a relative error of at most 0.0014.
Values sent between devices are 32-bit elements; how exact they have to be, the bound alone decides.
A program may use at most 128 MiB of HBM per device.

```python
import math
import jax
import jax.numpy as jnp
from jax import lax

NLON = 1440
NLAT = 720
MAXM = 720
LEV = 2
DAYS = 8
S = 16
SLOTS = 736


def draw_sample_level(key, part):
    order = jax.random.permutation(key, S)
    return (order % LEV).astype(jnp.int32)


def draw_slot_wavenumber(key, part):
    order = jax.random.permutation(key, SLOTS)
    return jnp.where(order < MAXM, order, -1).astype(jnp.int32)


def level_of(rng, dims, pieces, smallest, top_value):
    factor_of = 1.0
    for position, shards_of in pieces:
        draws = jax.random.uniform(jax.random.fold_in(jax.random.fold_in(rng, 6), position), (shards_of,), jnp.float32, smallest / len(pieces), top_value / len(pieces))
        factor_of = factor_of * jnp.repeat(jnp.exp(draws), dims[position] // shards_of).reshape((-1,) + (1,) * (len(dims) - 1 - position))
    return factor_of


def gaussian(stream_key, shape, deviation, reach, pieces=(), held_as=jnp.bfloat16):
    gain = level_of(stream_key, shape, pieces, -0.22, 0.18) if pieces else 1.0
    drawn = jax.random.normal(stream_key, shape, jnp.float32) * deviation * gain
    return jnp.minimum(jnp.maximum(drawn, -reach), reach).astype(held_as)


def setup_inputs(seed: int = 0) -> dict:
    streams_of = jax.random.split(jax.random.key(seed), 8)
    wind_u = gaussian(streams_of[0], (NLAT, NLON, S), 1.0, 6.0, ((0, 16), (1, 32)), jnp.float32)
    wind_v = gaussian(streams_of[1], (NLAT, NLON, S), 1.0, 6.0, ((0, 16), (1, 32)), jnp.float32)
    vorticity = gaussian(streams_of[2], (NLAT, NLON, S), 1.0, 6.0, ((0, 16), (1, 32)), jnp.float32)
    sample_level = draw_sample_level(jax.random.fold_in(streams_of[7], 71), 0)
    slot_wavenumber = draw_slot_wavenumber(jax.random.fold_in(streams_of[7], 71), 0)
    legendre_p = gaussian(streams_of[5], (NLAT, SLOTS * MAXM), 1.0, 5.0, ((0, 16), (1, 32)))
    legendre_h = gaussian(streams_of[6], (NLAT, SLOTS * MAXM), 1.0, 5.0, ((0, 16), (1, 32)))
    return dict(wind_u=wind_u, wind_v=wind_v, vorticity=vorticity, sample_level=sample_level, slot_wavenumber=slot_wavenumber, legendre_p=legendre_p, legendre_h=legendre_h)


def remove_means(field, onehot):
    means = jnp.einsum("jis,sl->jil", field, onehot, precision=lax.Precision.HIGHEST) / DAYS
    return field - jnp.einsum("jil,sl->jis", means, onehot, precision=lax.Precision.HIGHEST)


def reference(wind_u, wind_v, vorticity, sample_level, slot_wavenumber, legendre_p, legendre_h):
    onehot = (sample_level[:, None] == jnp.arange(LEV, dtype=jnp.int32)[None, :]).astype(jnp.float32)
    eddy_u = remove_means(wind_u, onehot)
    eddy_v = remove_means(wind_v, onehot)
    eddy_z = remove_means(vorticity, onehot)
    latitude = (jnp.arange(NLAT, dtype=jnp.float32) + 0.5) * (math.pi / NLAT) - 0.5 * math.pi
    cosine = jnp.cos(latitude)[:, None, None]
    fluxes = jnp.concatenate([eddy_u * eddy_z * cosine, eddy_v * eddy_z * cosine], axis=2)
    spectrum = jnp.fft.rfft(fluxes, axis=1) / NLON
    present = slot_wavenumber >= 0
    clipped = jnp.maximum(slot_wavenumber, 0).astype(jnp.int32)
    weight = present.astype(jnp.float32)[None, :, None]
    cos_part = jnp.real(spectrum)[:, clipped, :] * weight
    sin_part = -jnp.imag(spectrum)[:, clipped, :] * weight
    scale = (clipped.astype(jnp.float32) / MAXM)[None, :, None]
    right_p = jnp.concatenate([scale * sin_part[:, :, :S], scale * cos_part[:, :, :S]], axis=2).astype(jnp.bfloat16)
    right_h = jnp.concatenate([-cos_part[:, :, S:], sin_part[:, :, S:]], axis=2).astype(jnp.bfloat16)
    degree = jnp.arange(MAXM, dtype=jnp.int32)

    def per_slot(index):
        table_p = lax.dynamic_slice_in_dim(legendre_p, index * MAXM, MAXM, 1).astype(jnp.float32)
        table_h = lax.dynamic_slice_in_dim(legendre_h, index * MAXM, MAXM, 1).astype(jnp.float32)
        rhs_p = lax.dynamic_index_in_dim(right_p, index, 1, keepdims=False).astype(jnp.float32)
        rhs_h = lax.dynamic_index_in_dim(right_h, index, 1, keepdims=False).astype(jnp.float32)
        coeffs = jnp.dot(table_p.T, rhs_p, precision=lax.Precision.HIGHEST)
        coeffs = coeffs + jnp.dot(table_h.T, rhs_h, precision=lax.Precision.HIGHEST)
        keep = ((degree >= clipped[index]) & present[index]).astype(jnp.float32)
        coeffs = coeffs * keep[:, None]
        power = coeffs[:, :S] ** 2 + coeffs[:, S:] ** 2
        return jnp.dot(power, onehot, precision=lax.Precision.HIGHEST) / DAYS

    spectra = lax.map(per_slot, jnp.arange(SLOTS, dtype=jnp.int32))
    return spectra.reshape(SLOTS * MAXM, LEV).T
```

```python
import math

import jax
import jax.numpy as jnp
from jax import lax
from jax.experimental import pallas as pl
from jax.experimental.pallas import tpu as pltpu
from jax.sharding import PartitionSpec as P

NLON = 1440
NLAT = 720
MAXM = 720
LEV = 2
DAYS = 8
S = 16

LON = 32
LAT = 16
BAND = NLAT // LAT
LOCAL = NLON // LON
OWN = 23
ROWS = 24
COLS = OWN * MAXM
SHARE = COLS // LAT
WIDE = 1152
STEP = 11

F32 = jnp.float32
BF16 = jnp.bfloat16
MESH = pl.DeviceIdType.MESH


def iota(shape, dim):
    return lax.broadcasted_iota(jnp.int32, shape, dim)


def roll64(value):
    return pltpu.roll(value, 64, 1)


def sincos(turns):
    quarter = jnp.floor(turns * (1.0 / 360.0) + 0.5)
    phi = (turns - 360.0 * quarter) * (2.0 * math.pi / NLON)
    sq = phi * phi
    s = phi * (1.0 + sq * (-1.0 / 6 + sq * (1.0 / 120 + sq * (-1.0 / 5040 + sq * (1.0 / 362880)))))
    c = 1.0 + sq * (-0.5 + sq * (1.0 / 24 + sq * (-1.0 / 720 + sq * (1.0 / 40320 - sq * (1.0 / 3628800)))))
    quad = quarter.astype(jnp.int32) & 3
    odd = (quad & 1) == 1
    cos = jnp.where(odd, s, c)
    sin = jnp.where(odd, c, s)
    cos = jnp.where((quad == 1) | (quad == 2), -cos, cos)
    sin = jnp.where(quad >= 2, -sin, sin)
    return cos, sin


def kernel(
    u_ref, v_ref, z_ref, level_ref, wave_ref, p_hbm, h_hbm, out_ref,
    p_ref, h_ref, flux, send1, recv1, wsend, wrecv,
    cos_hi, cos_lo, sin_hi, sin_lo, xs, send2, recv2, left_p, left_h,
    total, toward, held, got_core, got_a, got_b, plus, minus, final, got_z,
    load_sem, wsend_sem, wrecv_sem, send1_sem, recv1_sem, send2_sem, recv2_sem,
    core_send, core_recv, x_send, x_recv, z_send, z_recv,
):
    me = lax.axis_index("lon")
    lat = lax.axis_index("lat")
    core = lax.rem(lat, 2)
    x = lax.rem(lat // 2, 4)
    half = lat // 8

    def lat_at(h, xx, cc):
        return (h * 4 + xx) * 2 + cc

    partner = lat_at(half, x, 1 - core)
    up = lat_at(half, lax.rem(x + 1, 4), core)
    down = lat_at(half, lax.rem(x + 3, 4), core)
    across = lat_at(1 - half, x, core)

    def other(k):
        return lax.rem(me + STEP * k, LON)

    load_p = pltpu.make_async_copy(p_hbm, p_ref, load_sem.at[0])
    load_h = pltpu.make_async_copy(h_hbm, h_ref, load_sem.at[1])
    load_p.start()
    load_h.start()
    barrier = pltpu.get_barrier_semaphore()

    def greet(k, carry):
        pl.semaphore_signal(barrier, inc=1, device_id=(other(k), lat), device_id_type=MESH)
        return carry

    lax.fori_loop(1, LON, greet, 0)
    for there in (partner, up, down, across):
        pl.semaphore_signal(barrier, inc=1, device_id=(me, there), device_id_type=MESH)

    rows16 = iota((S, 128), 0)
    upper = jnp.zeros((S, 128), F32)
    for s in range(S):
        upper = jnp.where(rows16 == s, level_ref[s].astype(F32), upper)
    lower = 1.0 - upper
    upper45 = upper[None, :, :LOCAL]
    lower45 = lower[None, :, :LOCAL]
    flux[pl.ds(BAND * 32, 96), :] = jnp.zeros((96, 128), F32)
    STRIP = 9

    def eddies(strip, carry):
        at = strip * STRIP

        def eddy(ref):
            field = ref[pl.ds(at, STRIP)]
            one = jnp.sum(field * upper45, axis=1, keepdims=True)
            zero = jnp.sum(field * lower45, axis=1, keepdims=True)
            return field - (one * upper45 + zero * lower45) * (1.0 / DAYS)

        row = lat * BAND + at + iota((STRIP, 1, LOCAL), 0)
        theta = (row.astype(F32) + 0.5) * (math.pi / NLAT) - 0.5 * math.pi
        ez = eddy(z_ref) * jnp.cos(theta)
        fu = eddy(u_ref) * ez
        fv = eddy(v_ref) * ez
        for j in range(STRIP):
            base = pl.multiple_of((at + j) * 32, 32)
            flux[pl.ds(base, S), 0:LOCAL] = fu[j]
            flux[pl.ds(base + S, S), 0:LOCAL] = fv[j]
        return carry

    lax.fori_loop(0, BAND // STRIP, eddies, 0)

    lane1 = iota((1, 128), 1)
    waves = jnp.full((1, 128), -1.0, F32)
    for q in range(OWN):
        waves = jnp.where(lane1 == q, wave_ref[q].astype(F32), waves)
    wsend[...] = waves
    wrecv[me] = waves

    pl.semaphore_wait(barrier, LON - 1 + 4)

    def wave_copy(k, there):
        return pltpu.make_async_remote_copy(
            src_ref=wsend, dst_ref=wrecv.at[me],
            send_sem=wsend_sem.at[k], recv_sem=wrecv_sem.at[me],
            device_id=(there, lat), device_id_type=MESH,
        )

    def wave_start(k, carry):
        wave_copy(k, other(k)).start()
        return carry

    lax.fori_loop(1, LON, wave_start, 0)

    lane24 = iota((ROWS, 128), 1)
    low24 = lane24 < 64

    def message(c):
        first = flux[pl.ds(c, ROWS, stride=32), :]
        second = flux[pl.ds(c + ROWS * 32, ROWS, stride=32), :]
        packed = jnp.where(low24, first, roll64(second))
        return jnp.where((lane24 & 63) < LOCAL, packed, 0.0)

    def block(c):
        return pl.ds(pl.multiple_of(c * ROWS, 8), ROWS)

    def copy1(k, there):
        return pltpu.make_async_remote_copy(
            src_ref=send1.at[block(k)], dst_ref=recv1.at[block(me)],
            send_sem=send1_sem.at[k], recv_sem=recv1_sem.at[me],
            device_id=(there, lat), device_id_type=MESH,
        )

    def start1(k, carry):
        c = other(k)
        send1[block(k), :] = message(c)
        copy1(k, c).start()
        return carry

    lax.fori_loop(1, LON, start1, 0)
    recv1[block(me), :] = message(me)

    def wave_wait(k, carry):
        s = other(k)
        pltpu.make_async_remote_copy(
            src_ref=wsend, dst_ref=wrecv.at[s],
            send_sem=wsend_sem.at[k], recv_sem=wrecv_sem.at[s],
            device_id=(s, lat), device_id_type=MESH,
        ).wait()
        return carry

    lax.fori_loop(1, LON, wave_wait, 0)

    on_diagonal = iota((ROWS, 128), 0) == lane24

    def wave_column(s):
        row = jnp.broadcast_to(wrecv[s], (ROWS, 128))
        return jnp.sum(jnp.where(on_diagonal, row, 0.0), axis=1, keepdims=True)

    def split(value):
        high = value.astype(BF16)
        return high, (value - high.astype(F32)).astype(BF16)

    lane48 = iota((2 * ROWS, 128), 1)
    lon48 = ((lane48 & 63) + jnp.where(lane48 < 64, 0, LOCAL)).astype(F32)

    def tables(pair, carry):
        wave = jnp.concatenate([wave_column(2 * pair), wave_column(2 * pair + 1)], axis=0)
        wave = jnp.maximum(wave, 0.0)
        c, s = sincos(wave * lon48)
        rc, rs = sincos(jnp.broadcast_to(wave * (2.0 * LOCAL), (2 * ROWS, 128)))
        at = pl.ds(pl.multiple_of(pair * 2 * ROWS, 16), 2 * ROWS)
        for j in range(8):
            lanes = slice(128 * j, 128 * (j + 1))
            ch, cl = split(c)
            sh, sl = split(s)
            cos_hi[at, lanes] = ch
            cos_lo[at, lanes] = cl
            sin_hi[at, lanes] = sh
            sin_lo[at, lanes] = sl
            c, s = c * rc - s * rs, s * rc + c * rs
        return carry

    lax.fori_loop(0, LON // 2, tables, 0)

    def wait1(k, carry):
        s = other(k)
        pltpu.make_async_remote_copy(
            src_ref=send1.at[block(k)], dst_ref=recv1.at[block(s)],
            send_sem=send1_sem.at[k], recv_sem=recv1_sem.at[s],
            device_id=(s, lat), device_id_type=MESH,
        ).wait()
        return carry

    lax.fori_loop(1, LON, wait1, 0)

    pad = jnp.zeros((16, 128), F32)
    for h in range(2):
        for j in range(8):
            a = recv1[ROWS * (16 * h + 2 * j):ROWS * (16 * h + 2 * j + 1), :]
            b = recv1[ROWS * (16 * h + 2 * j + 1):ROWS * (16 * h + 2 * j + 2), :]
            piece = jnp.concatenate(
                [jnp.where(low24, a, roll64(b)), jnp.where(low24, roll64(a), b), pad], axis=0
            )
            high, low = split(piece)
            xs[64 * h:64 * h + 64, 128 * j:128 * (j + 1)] = high
            xs[128 + 64 * h:192 + 64 * h, 128 * j:128 * (j + 1)] = low

    is_v = me >= S
    nt = (((1,), (1,)), ((), ()))
    PART = 384
    lane_part = iota((PART, 128), 1)
    low_part = lane_part < 64

    def copy2(k, there):
        return pltpu.make_async_remote_copy(
            src_ref=send2.at[block(there)], dst_ref=recv2.at[block(me)],
            send_sem=send2_sem.at[k], recv_sem=recv2_sem.at[me],
            device_id=(there, lat), device_id_type=MESH,
        )

    for part in range(LON * ROWS // PART):
        at = slice(part * PART, (part + 1) * PART)

        def transform(high_ref, low_ref):
            wide = lax.dot_general(high_ref[at, :], xs[...], nt, preferred_element_type=F32)
            thin = lax.dot_general(low_ref[at, :], xs[0:128, :], nt, preferred_element_type=F32)
            return wide[:, :128] + wide[:, 128:] + thin

        c = transform(cos_hi, cos_lo)
        s = transform(sin_hi, sin_lo)
        wave = jnp.concatenate(
            [wave_column(i) for i in range(part * PART // ROWS, (part + 1) * PART // ROWS)], axis=0
        )
        clipped = jnp.maximum(wave, 0.0)
        present = jnp.where(wave >= 0.0, 1.0 / NLON, 0.0)
        sign = 1.0 - 2.0 * (clipped - 2.0 * jnp.floor(clipped * 0.5))
        scale = clipped * (1.0 / MAXM) * present
        sin_scale = jnp.where(is_v, present, scale)
        cos_scale = jnp.where(is_v, -present, scale)
        near = jnp.where(low_part, s, roll64(c))
        far = jnp.where(low_part, roll64(s), c)
        near = jnp.where(low_part, s, roll64(c))
        send2[at, :] = (near + sign * far) * jnp.where(low_part, sin_scale, cos_scale)

    def start2(k, carry):
        copy2(k, other(k)).start()
        return carry

    lax.fori_loop(1, LON, start2, 0)
    recv2[block(me), :] = send2[block(me), :]

    def wait2(k, carry):
        s = other(k)
        pltpu.make_async_remote_copy(
            src_ref=send2.at[block(s)], dst_ref=recv2.at[block(s)],
            send_sem=send2_sem.at[k], recv_sem=recv2_sem.at[s],
            device_id=(s, lat), device_id_type=MESH,
        ).wait()
        return carry

    lax.fori_loop(1, LON, wait2, 0)

    def sides(q, carry):
        wu = recv2[pl.ds(q, S, stride=ROWS), :]
        wv = recv2[pl.ds(q + S * ROWS, S, stride=ROWS), :]
        at = pl.ds(pl.multiple_of(q * 32, 32), 32)
        left_p[at, :] = jnp.concatenate([wu, roll64(wu)], axis=0).astype(BF16)
        left_h[at, :] = jnp.concatenate([roll64(wv), wv], axis=0).astype(BF16)
        return carry

    lax.fori_loop(0, ROWS, sides, 0)
    load_p.wait()
    load_h.wait()

    def legendre(base, q, cols):
        rows = pl.ds(pl.multiple_of(q * 32, 32), 64)
        r = jnp.dot(left_p[rows, 0:BAND], p_ref[:, cols], preferred_element_type=F32)
        r = r + jnp.dot(left_h[rows, 0:BAND], h_ref[:, cols], preferred_element_type=F32)
        inside = iota((32, r.shape[1]), 1) < MAXM * (q + 1) - base
        return jnp.where(inside, r[:32], r[32:])

    TILE = 256

    def sums(t, carry):
        base = t * TILE
        cols = pl.ds(pl.multiple_of(base, TILE), TILE)
        total[:, cols] = legendre(base, base // MAXM, cols)
        return carry

    whole = COLS // TILE
    lax.fori_loop(0, whole, sums, 0, unroll=4)
    last = slice(whole * TILE, COLS)
    total[:, last] = legendre(whole * TILE, OWN - 1, last)

    lane32 = iota((32, 128), 1)

    def chunk(b):
        first = SHARE * b
        tile = first // 128
        shift = first - tile * 128
        back = lax.rem(128 - shift, 128)
        inside = lane32 < 128 - shift
        turned = [
            pltpu.roll(total[:, pl.ds(pl.multiple_of((tile + i) * 128, 128), 128)], back, 1)
            for i in range(10)
        ]
        return [jnp.where(inside, turned[i], turned[i + 1]) for i in range(9)]

    order = [(1, 2), (1, 1), (1, 3), (1, 0), (0, 2), (0, 1), (0, 3), (0, 0)]
    place = {pair: i for i, pair in enumerate(order)}

    def target(pair, cc):
        dz, dx = pair
        return lat_at(half if dz == 0 else 1 - half, lax.rem(x + dx, 4), cc)

    def send(src, dst, sends, recvs, i, there):
        return pltpu.make_async_remote_copy(
            src_ref=src, dst_ref=dst, send_sem=sends.at[i], recv_sem=recvs.at[i],
            device_id=(me, there), device_id_type=MESH,
        )

    core_copies = []
    for i, pair in enumerate(order):
        pieces = chunk(target(pair, 1 - core))
        for n in range(9):
            toward[i, :, 128 * n:128 * (n + 1)] = pieces[n]
        copy = send(toward.at[i], got_core.at[i], core_send, core_recv, i, partner)
        copy.start()
        core_copies.append(copy)

    A, B = slice(0, 16), slice(16, 32)
    x_copies = {}

    def x_start(i, src, dst, there):
        copy = send(src, dst, x_send, x_recv, i, there)
        copy.start()
        x_copies[i] = copy

    def merge(pair):
        i = place[pair]
        pieces = chunk(target(pair, core))
        core_copies[i].wait()
        for n in range(9):
            lanes = slice(128 * n, 128 * (n + 1))
            held[i, :, lanes] = pieces[n] + got_core[i, :, lanes]

    for dz in (1, 0):
        k = 6 * dz
        merge((dz, 2))
        i = place[(dz, 2)]
        x_start(k, held.at[i, A], got_a.at[dz], up)
        x_start(k + 1, held.at[i, B], got_b.at[dz], down)
        merge((dz, 1))
        x_start(k + 2, held.at[place[(dz, 1)], B], plus.at[dz, B], up)
        merge((dz, 3))
        x_start(k + 3, held.at[place[(dz, 3)], A], minus.at[dz, A], down)
        merge((dz, 0))
    z_copies = []
    for dz in (1, 0):
        k = 6 * dz
        i, j, own = place[(dz, 1)], place[(dz, 3)], place[(dz, 0)]
        x_copies[k].wait()
        held[i, A] = held[i, A] + got_a[dz]
        x_start(k + 4, held.at[i, A], plus.at[dz, A], up)
        x_copies[k + 1].wait()
        held[j, B] = held[j, B] + got_b[dz]
        x_start(k + 5, held.at[j, B], minus.at[dz, B], down)
    for dz in (1, 0):
        k = 6 * dz
        own = place[(dz, 0)]
        x_copies[k + 4].wait()
        x_copies[k + 3].wait()
        final[dz, A] = held[own, A] + plus[dz, A] + minus[dz, A]
        if dz == 1:
            copy = send(final.at[1, A], got_z.at[A], z_send, z_recv, 0, across)
            copy.start()
            z_copies.append(copy)
        x_copies[k + 5].wait()
        x_copies[k + 2].wait()
        final[dz, B] = held[own, B] + plus[dz, B] + minus[dz, B]
        if dz == 1:
            copy = send(final.at[1, B], got_z.at[B], z_send, z_recv, 1, across)
            copy.start()
            z_copies.append(copy)
    for copy in z_copies:
        copy.wait()

    first = lat * SHARE
    slot = first // MAXM
    lane = first + iota((1, WIDE), 1)
    keep = jnp.zeros((1, WIDE), F32)
    for d in range(3):
        q = jnp.minimum(slot + d, OWN - 1)
        wave = wave_ref[q]
        n = lane - (slot + d) * MAXM
        good = (n >= 0) & (n < MAXM) & (n >= wave) & (wave >= 0)
        keep = jnp.where(good, 1.0, keep)
    re = final[0, A] + got_z[A]
    im = final[0, B] + got_z[B]
    power = re * re + im * im
    one = jnp.sum(power * upper[:, :1], axis=0, keepdims=True)
    zero = jnp.sum(power * lower[:, :1], axis=0, keepdims=True)
    keep = keep * (1.0 / DAYS)
    out_ref[0:1, :] = (zero * keep)[:, :SHARE]
    out_ref[1:2, :] = (one * keep)[:, :SHARE]


def body(wind_u, wind_v, vorticity, sample_level, slot_wavenumber, legendre_p, legendre_h):
    def turned(field):
        return jnp.transpose(field, (0, 2, 1))

    vmem = pl.BlockSpec(memory_space=pltpu.VMEM)
    smem = pl.BlockSpec(memory_space=pltpu.SMEM)
    hbm = pl.BlockSpec(memory_space=pl.ANY)
    dma = pltpu.SemaphoreType.DMA
    scratch = [
        pltpu.VMEM((BAND, COLS), BF16),
        pltpu.VMEM((BAND, COLS), BF16),
        pltpu.VMEM((48 * 32, 128), F32),
        pltpu.VMEM((LON * ROWS, 128), F32),
        pltpu.VMEM((LON * ROWS, 128), F32),
        pltpu.VMEM((1, 128), F32),
        pltpu.VMEM((LON, 1, 128), F32),
        pltpu.VMEM((LON * ROWS, 1024), BF16),
        pltpu.VMEM((LON * ROWS, 1024), BF16),
        pltpu.VMEM((LON * ROWS, 1024), BF16),
        pltpu.VMEM((LON * ROWS, 1024), BF16),
        pltpu.VMEM((256, 1024), BF16),
        pltpu.VMEM((LON * ROWS, 128), F32),
        pltpu.VMEM((LON * ROWS, 128), F32),
        pltpu.VMEM((ROWS * 32, 128), BF16),
        pltpu.VMEM((ROWS * 32, 128), BF16),
        pltpu.VMEM((32, 131 * 128), F32),
        pltpu.VMEM((8, 32, WIDE), F32),
        pltpu.VMEM((8, 32, WIDE), F32),
        pltpu.VMEM((8, 32, WIDE), F32),
        pltpu.VMEM((2, 16, WIDE), F32),
        pltpu.VMEM((2, 16, WIDE), F32),
        pltpu.VMEM((2, 32, WIDE), F32),
        pltpu.VMEM((2, 32, WIDE), F32),
        pltpu.VMEM((2, 32, WIDE), F32),
        pltpu.VMEM((32, WIDE), F32),
        dma((2,)),
        dma((LON,)), dma((LON,)), dma((LON,)), dma((LON,)), dma((LON,)), dma((LON,)),
        dma((8,)), dma((8,)), dma((12,)), dma((12,)), dma((2,)), dma((2,)),
    ]
    return pl.pallas_call(
        kernel,
        out_shape=jax.ShapeDtypeStruct((LEV, SHARE), F32),
        in_specs=[vmem, vmem, vmem, smem, smem, hbm, hbm],
        out_specs=vmem,
        scratch_shapes=scratch,
        compiler_params=pltpu.CompilerParams(
            collective_id=0, has_side_effects=True, vmem_limit_bytes=60 * 1024 * 1024
        ),
    )(turned(wind_u), turned(wind_v), turned(vorticity), sample_level, slot_wavenumber,
      legendre_p, legendre_h)


def solution(mesh):
    placed = (
        P("lat", "lon", None),
        P("lat", "lon", None),
        P("lat", "lon", None),
        P(),
        P("lon"),
        P("lat", "lon"),
        P("lat", "lon"),
    )
    return jax.shard_map(
        body, mesh=mesh, in_specs=placed, out_specs=P(None, ("lon", "lat")), check_vma=False
    )
```

```python
import math

import jax
import jax.numpy as jnp
from jax import lax
from jax.experimental import pallas as pl
from jax.experimental.pallas import tpu as pltpu
from jax.sharding import PartitionSpec as P

NLON = 1440
NLAT = 720
MAXM = 720
LEV = 2
DAYS = 8
S = 16

LON = 32
LAT = 16
BAND = NLAT // LAT
LOCAL = NLON // LON
OWN = 23
IN_ROWS = 16
OUT_ROWS = 17
SPACE = 24
COLS = OWN * MAXM
SHARE = COLS // LAT
WIDE = 1152
STEP = 11

F32 = jnp.float32
BF16 = jnp.bfloat16
MESH = pl.DeviceIdType.MESH


def iota(shape, dim):
    return lax.broadcasted_iota(jnp.int32, shape, dim)


def roll64(value):
    return pltpu.roll(value, 64, 1)


def sincos(turns):
    quarter = jnp.floor(turns * (1.0 / 360.0) + 0.5)
    phi = (turns - 360.0 * quarter) * (2.0 * math.pi / NLON)
    sq = phi * phi
    s = phi * (1.0 + sq * (-1.0 / 6 + sq * (1.0 / 120 + sq * (-1.0 / 5040 + sq * (1.0 / 362880)))))
    c = 1.0 + sq * (-0.5 + sq * (1.0 / 24 + sq * (-1.0 / 720 + sq * (1.0 / 40320 - sq * (1.0 / 3628800)))))
    quad = quarter.astype(jnp.int32) & 3
    odd = (quad & 1) == 1
    cos = jnp.where(odd, s, c)
    sin = jnp.where(odd, c, s)
    cos = jnp.where((quad == 1) | (quad == 2), -cos, cos)
    sin = jnp.where(quad >= 2, -sin, sin)
    return cos, sin


def packed(source, blocks, j):
    lane = iota((32, 128), 1)
    tile = jnp.zeros((32, 128), F32)
    for t in range(blocks):
        at = t * BAND - 128 * j
        if at >= 128 or at + BAND <= 0:
            continue
        value, start = source(t)
        shift = (at - start) % 128
        value = pltpu.roll(value, shift, 1) if shift else value
        tile = jnp.where((lane >= at) & (lane < at + BAND), value, tile)
    return tile


def unpacked(tile, t):
    lane = iota((32, 128), 1)
    j, at = divmod(t * BAND, 128)
    if at == 0:
        return tile(j)
    value = pltpu.roll(tile(j), 128 - at, 1)
    if at + BAND > 128:
        value = jnp.where(lane < 128 - at, value, pltpu.roll(tile(j + 1), 128 - at, 1))
    return value


def kernel(
    u_ref, v_ref, z_ref, level_ref, wave_ref, p_hbm, h_hbm, out_ref,
    p_ref, h_ref, wide_p, wide_h, flux, row1, send1, recv1, wsend, wrecv,
    cos_hi, cos_lo, sin_hi, sin_lo, field, xs, coeff, row2, send2, recv2, left_p, left_h,
    toward, held, got_core, got_a, got_b, plus, minus, final, got_z,
    load_sem, wsend_sem, wrecv_sem, send1_sem, recv1_sem, send2_sem, recv2_sem,
    core_send, core_recv, x_send, x_recv, z_send, z_recv,
):
    me = lax.axis_index("lon")
    lat = lax.axis_index("lat")
    core = lax.rem(lat, 2)
    x = lax.rem(lat // 2, 4)
    half = lat // 8

    def lat_at(h, xx, cc):
        return (h * 4 + xx) * 2 + cc

    partner = lat_at(half, x, 1 - core)
    up = lat_at(half, lax.rem(x + 1, 4), core)
    down = lat_at(half, lax.rem(x + 3, 4), core)
    across = lat_at(1 - half, x, core)

    def other(k):
        return lax.rem(me + STEP * k, LON)

    load_p = pltpu.make_async_copy(p_hbm, p_ref, load_sem.at[0])
    load_h = pltpu.make_async_copy(h_hbm, h_ref, load_sem.at[1])
    load_p.start()
    load_h.start()
    barrier = pltpu.get_barrier_semaphore()

    def greet(k, carry):
        pl.semaphore_signal(barrier, inc=1, device_id=(other(k), lat), device_id_type=MESH)
        return carry

    lax.fori_loop(1, LON, greet, 0)
    for there in (partner, up, down, across):
        pl.semaphore_signal(barrier, inc=1, device_id=(me, there), device_id_type=MESH)

    rows16 = iota((S, 128), 0)
    upper = jnp.zeros((S, 128), F32)
    for s in range(S):
        upper = jnp.where(rows16 == s, level_ref[s].astype(F32), upper)
    lower = 1.0 - upper
    upper45 = upper[None, :, :LOCAL]
    lower45 = lower[None, :, :LOCAL]
    STRIP = 9

    def eddies(strip, carry):
        at = strip * STRIP

        def eddy(ref):
            value = ref[pl.ds(at, STRIP)]
            one = jnp.sum(value * upper45, axis=1, keepdims=True)
            zero = jnp.sum(value * lower45, axis=1, keepdims=True)
            return value - (one * upper45 + zero * lower45) * (1.0 / DAYS)

        row = lat * BAND + at + iota((STRIP, 1, LOCAL), 0)
        theta = (row.astype(F32) + 0.5) * (math.pi / NLAT) - 0.5 * math.pi
        ez = eddy(z_ref) * jnp.cos(theta)
        fu = eddy(u_ref) * ez
        fv = eddy(v_ref) * ez
        for j in range(STRIP):
            base = pl.multiple_of((at + j) * 32, 32)
            flux[pl.ds(base, S), 0:LOCAL] = fu[j]
            flux[pl.ds(base + S, S), 0:LOCAL] = fv[j]
        return carry

    lax.fori_loop(0, BAND // STRIP, eddies, 0)

    for j in range(IN_ROWS):
        row1[32 * j:32 * j + 32, :] = packed(lambda t: (flux[32 * t:32 * t + 32, :], 0), BAND, j)

    lane1 = iota((1, 128), 1)
    waves = jnp.full((1, 128), -1.0, F32)
    for q in range(OWN):
        waves = jnp.where(lane1 == q, wave_ref[q].astype(F32), waves)
    wsend[...] = waves
    wrecv[pl.ds(me, 1), :] = waves

    pl.semaphore_wait(barrier, LON - 1 + 4)

    def wave_copy(k, there, source):
        return pltpu.make_async_remote_copy(
            src_ref=wsend, dst_ref=wrecv.at[pl.ds(source, 1)],
            send_sem=wsend_sem.at[k], recv_sem=wrecv_sem.at[source],
            device_id=(there, lat), device_id_type=MESH,
        )

    def wave_start(k, carry):
        wave_copy(k, other(k), me).start()
        return carry

    lax.fori_loop(1, LON, wave_start, 0)

    def in_block(c):
        return pl.ds(pl.multiple_of(c * IN_ROWS, 8), IN_ROWS)

    def copy1(k, there, source):
        return pltpu.make_async_remote_copy(
            src_ref=send1.at[in_block(k)], dst_ref=recv1.at[in_block(source)],
            send_sem=send1_sem.at[k], recv_sem=recv1_sem.at[source],
            device_id=(there, lat), device_id_type=MESH,
        )

    def start1(k, carry):
        c = other(k)
        send1[in_block(k), :] = row1[pl.ds(c, IN_ROWS, stride=32), :]
        copy1(k, c, me).start()
        return carry

    lax.fori_loop(1, LON, start1, 0)
    recv1[in_block(me), :] = row1[pl.ds(me, IN_ROWS, stride=32), :]

    load_p.wait()
    load_h.wait()
    PIECE = 2048

    def widen(i, carry):
        cols = pl.ds(pl.multiple_of(i * PIECE, PIECE), PIECE)
        wide_p[:, cols] = p_ref[:, cols]
        wide_h[:, cols] = h_ref[:, cols]
        return carry

    lax.fori_loop(0, COLS // PIECE, widen, 0)
    rest = slice(COLS // PIECE * PIECE, COLS)
    wide_p[:, rest] = p_ref[:, rest]
    wide_h[:, rest] = h_ref[:, rest]

    def wave_wait(k, carry):
        wave_copy(k, other(k), other(k)).wait()
        return carry

    lax.fori_loop(1, LON, wave_wait, 0)
    lane32 = iota((32, 128), 1)

    def wave_column(q):
        return jnp.sum(jnp.where(lane32 == q, wrecv[...], 0.0), axis=1, keepdims=True)

    def split(value):
        high = value.astype(BF16)
        return high, (value - high.astype(F32)).astype(BF16)

    lon32 = ((lane32 & 63) + jnp.where(lane32 < 64, 0, LOCAL)).astype(F32)

    def tables(q, carry):
        wave = jnp.maximum(wave_column(q), 0.0)
        c, s = sincos(wave * lon32)
        rc, rs = sincos(jnp.broadcast_to(wave * (2.0 * LOCAL), (32, 128)))
        at = pl.ds(pl.multiple_of(q * 32, 32), 32)
        for j in range(8):
            lanes = slice(128 * j, 128 * (j + 1))
            ch, cl = split(c)
            sh, sl = split(s)
            cos_hi[at, lanes] = ch
            cos_lo[at, lanes] = cl
            sin_hi[at, lanes] = sh
            sin_lo[at, lanes] = sl
            c, s = c * rc - s * rs, s * rc + c * rs
        return carry

    lax.fori_loop(0, OWN, tables, 0)

    def wait1(k, carry):
        copy1(k, other(k), other(k)).wait()
        return carry

    lax.fori_loop(1, LON, wait1, 0)

    row_tile = {}

    def in_tile(j):
        if j not in row_tile:
            row_tile[j] = recv1[pl.ds(j, LON, stride=IN_ROWS), :]
        return row_tile[j]

    for t in range(BAND):
        field[pl.ds(t, LON, stride=48), :] = unpacked(in_tile, t)

    lane48 = iota((48, 128), 1)
    west = lane48 < LOCAL
    east = (lane48 >= 64) & (lane48 < 64 + LOCAL)
    for h in range(2):
        for j in range(8):
            s = 16 * h + 2 * j
            a = field[48 * s:48 * s + 48, :]
            b = field[48 * s + 48:48 * s + 96, :]
            high, low = split(jnp.where(west, a, jnp.where(east, roll64(b), 0.0)))
            lanes = slice(128 * j, 128 * (j + 1))
            xs[64 * h:64 * h + 48, lanes] = high
            xs[128 + 64 * h:176 + 64 * h, lanes] = low

    is_v = me >= S
    nt = (((1,), (1,)), ((), ()))
    for first, count in ((0, 8), (8, 8), (16, 7)):
        size = count * 32
        at = slice(first * 32, first * 32 + size)
        low_part = iota((size, 128), 1) < 64

        def transform(high_ref, low_ref):
            wide = lax.dot_general(high_ref[at, :], xs[...], nt, preferred_element_type=F32)
            thin = lax.dot_general(low_ref[at, :], xs[0:128, :], nt, preferred_element_type=F32)
            return wide[:, :128] + wide[:, 128:] + thin

        c = transform(cos_hi, cos_lo)
        s = transform(sin_hi, sin_lo)
        wave = jnp.concatenate([wave_column(q) for q in range(first, first + count)], axis=0)
        clipped = jnp.maximum(wave, 0.0)
        present = jnp.where(wave >= 0.0, 1.0 / NLON, 0.0)
        sign = 1.0 - 2.0 * (clipped - 2.0 * jnp.floor(clipped * 0.5))
        scale = clipped * (1.0 / MAXM) * present
        sin_scale = jnp.where(is_v, present, scale)
        cos_scale = jnp.where(is_v, -present, scale)
        near = jnp.where(low_part, s, roll64(c))
        far = jnp.where(low_part, roll64(s), c)
        coeff[at, :] = (near + sign * far) * jnp.where(low_part, sin_scale, cos_scale)

    for j in range(OUT_ROWS):
        row2[32 * j:32 * j + 32, :] = packed(
            lambda t: (coeff[32 * (t // 2):32 * (t // 2) + 32, :], 64 * (t % 2)), 2 * OWN, j
        )

    def out_block(c):
        return pl.ds(pl.multiple_of(c * SPACE, 8), OUT_ROWS)

    def copy2(k, there, source):
        return pltpu.make_async_remote_copy(
            src_ref=send2.at[out_block(k)], dst_ref=recv2.at[out_block(source)],
            send_sem=send2_sem.at[k], recv_sem=recv2_sem.at[source],
            device_id=(there, lat), device_id_type=MESH,
        )

    def start2(k, carry):
        o = other(k)
        send2[out_block(k), :] = row2[pl.ds(o, OUT_ROWS, stride=32), :]
        copy2(k, o, me).start()
        return carry

    lax.fori_loop(1, LON, start2, 0)
    recv2[out_block(me), :] = row2[pl.ds(me, OUT_ROWS, stride=32), :]

    def wait2(k, carry):
        copy2(k, other(k), other(k)).wait()
        return carry

    lax.fori_loop(1, LON, wait2, 0)

    out_tiles = {}

    def out_tile(j):
        if j not in out_tiles:
            out_tiles[j] = recv2[pl.ds(j, LON, stride=SPACE), :]
        return out_tiles[j]

    for q in range(OWN):
        sin = unpacked(out_tile, 2 * q).astype(BF16)
        cos = unpacked(out_tile, 2 * q + 1).astype(BF16)
        at = slice(32 * q, 32 * q + 32)
        left_p[at, :] = jnp.concatenate([sin[:S], cos[:S]], axis=0)
        left_h[at, :] = jnp.concatenate([cos[S:], sin[S:]], axis=0)

    lane256 = iota((32, 256), 1)

    def chunk(b):
        first = SHARE * b
        tile = first // 128
        shift = first - tile * 128
        back = lax.rem(128 - shift, 128)
        inside = lane32 < 128 - shift
        turned = []
        for i in range(5):
            base = tile * 128 + 256 * i
            q = base // MAXM
            rows = pl.ds(pl.multiple_of(q * 32, 32), 64)
            cols = pl.ds(pl.multiple_of(base, 128), 256)
            r = jnp.dot(left_p[rows, 0:BAND], wide_p[:, cols], preferred_element_type=F32)
            r = r + jnp.dot(left_h[rows, 0:BAND], wide_h[:, cols], preferred_element_type=F32)
            r = jnp.where(lane256 < MAXM * (q + 1) - base, r[:32], r[32:])
            turned += [pltpu.roll(r[:, :128], back, 1), pltpu.roll(r[:, 128:], back, 1)]
        return [jnp.where(inside, turned[i], turned[i + 1]) for i in range(9)]

    order = [(1, 2), (1, 1), (1, 3), (0, 2), (1, 0), (0, 1), (0, 3), (0, 0)]
    place = {pair: i for i, pair in enumerate(order)}

    def target(pair, cc):
        dz, dx = pair
        return lat_at(half if dz == 0 else 1 - half, lax.rem(x + dx, 4), cc)

    def send(src, dst, sends, recvs, i, there):
        return pltpu.make_async_remote_copy(
            src_ref=src, dst_ref=dst, send_sem=sends.at[i], recv_sem=recvs.at[i],
            device_id=(me, there), device_id_type=MESH,
        )

    core_copies = {}

    def give(i):
        pieces = chunk(target(order[i], 1 - core))
        for n in range(9):
            toward[i, :, 128 * n:128 * (n + 1)] = pieces[n]
        core_copies[i] = send(toward.at[i], got_core.at[i], core_send, core_recv, i, partner)
        core_copies[i].start()

    def keep_own(i):
        pieces = chunk(target(order[i], core))
        for n in range(9):
            held[i, :, 128 * n:128 * (n + 1)] = pieces[n]

    def merge(i):
        core_copies[i].wait()
        held[i] = held[i] + got_core[i]

    A, B = slice(0, 16), slice(16, 32)
    x_copies = {}

    def x_start(i, src, dst, there):
        x_copies[i] = send(src, dst, x_send, x_recv, i, there)
        x_copies[i].start()

    def far_start(dz):
        i = place[(dz, 2)]
        x_start(6 * dz, held.at[i, A], got_a.at[dz], up)
        x_start(6 * dz + 1, held.at[i, B], got_b.at[dz], down)

    def near_start(dz):
        x_start(6 * dz + 2, held.at[place[(dz, 1)], B], plus.at[dz, B], up)
        x_start(6 * dz + 3, held.at[place[(dz, 3)], A], minus.at[dz, A], down)

    def relay(dz):
        i, j = place[(dz, 1)], place[(dz, 3)]
        x_copies[6 * dz].wait()
        held[i, A] = held[i, A] + got_a[dz]
        x_start(6 * dz + 4, held.at[i, A], plus.at[dz, A], up)
        x_copies[6 * dz + 1].wait()
        held[j, B] = held[j, B] + got_b[dz]
        x_start(6 * dz + 5, held.at[j, B], minus.at[dz, B], down)

    def finish(dz, part, one, two):
        own = place[(dz, 0)]
        x_copies[6 * dz + one].wait()
        x_copies[6 * dz + two].wait()
        final[dz, part] = held[own, part] + plus[dz, part] + minus[dz, part]

    for i in range(4):
        give(i)
    keep_own(0)
    merge(0)
    far_start(1)
    keep_own(1)
    merge(1)
    keep_own(2)
    merge(2)
    near_start(1)
    for i in range(4, 8):
        give(i)
    keep_own(3)
    keep_own(4)
    relay(1)
    merge(3)
    far_start(0)
    merge(4)
    keep_own(5)
    merge(5)
    keep_own(6)
    merge(6)
    near_start(0)
    keep_own(7)
    merge(7)
    finish(1, A, 3, 4)
    z_a = send(final.at[1, A], got_z.at[A], z_send, z_recv, 0, across)
    z_a.start()
    finish(1, B, 2, 5)
    z_b = send(final.at[1, B], got_z.at[B], z_send, z_recv, 1, across)
    z_b.start()
    relay(0)
    finish(0, A, 3, 4)
    finish(0, B, 2, 5)

    first = lat * SHARE
    slot = first // MAXM
    lane = first + iota((1, WIDE), 1)
    keep = jnp.zeros((1, WIDE), F32)
    for d in range(3):
        q = jnp.minimum(slot + d, OWN - 1)
        wave = wave_ref[q]
        n = lane - (slot + d) * MAXM
        good = (n >= 0) & (n < MAXM) & (n >= wave) & (wave >= 0)
        keep = jnp.where(good, 1.0 / DAYS, keep)
    z_a.wait()
    re = final[0, A] + got_z[A]
    z_b.wait()
    im = final[0, B] + got_z[B]
    power = re * re + im * im
    one = jnp.sum(power * upper[:, :1], axis=0, keepdims=True)
    zero = jnp.sum(power * lower[:, :1], axis=0, keepdims=True)
    out_ref[0:1, :] = (zero * keep)[:, :SHARE]
    out_ref[1:2, :] = (one * keep)[:, :SHARE]


def body(wind_u, wind_v, vorticity, sample_level, slot_wavenumber, legendre_p, legendre_h):
    def turned(field):
        return jnp.transpose(field, (0, 2, 1))

    vmem = pl.BlockSpec(memory_space=pltpu.VMEM)
    smem = pl.BlockSpec(memory_space=pltpu.SMEM)
    hbm = pl.BlockSpec(memory_space=pl.ANY)
    dma = pltpu.SemaphoreType.DMA
    scratch = [
        pltpu.VMEM((BAND, COLS), BF16),
        pltpu.VMEM((BAND, COLS), BF16),
        pltpu.VMEM((BAND, 131 * 128), BF16),
        pltpu.VMEM((BAND, 131 * 128), BF16),
        pltpu.VMEM((BAND * 32, 128), F32),
        pltpu.VMEM((IN_ROWS * 32, 128), F32),
        pltpu.VMEM((LON * IN_ROWS, 128), F32),
        pltpu.VMEM((LON * IN_ROWS, 128), F32),
        pltpu.VMEM((1, 128), F32),
        pltpu.VMEM((LON, 128), F32),
        pltpu.VMEM((OWN * 32, 1024), BF16),
        pltpu.VMEM((OWN * 32, 1024), BF16),
        pltpu.VMEM((OWN * 32, 1024), BF16),
        pltpu.VMEM((OWN * 32, 1024), BF16),
        pltpu.VMEM((LON * 48, 128), F32),
        pltpu.VMEM((256, 1024), BF16),
        pltpu.VMEM((OWN * 32, 128), F32),
        pltpu.VMEM((OUT_ROWS * 32, 128), F32),
        pltpu.VMEM((LON * SPACE, 128), F32),
        pltpu.VMEM((LON * SPACE, 128), F32),
        pltpu.VMEM(((OWN + 1) * 32, 128), BF16),
        pltpu.VMEM(((OWN + 1) * 32, 128), BF16),
        pltpu.VMEM((8, 32, WIDE), F32),
        pltpu.VMEM((8, 32, WIDE), F32),
        pltpu.VMEM((8, 32, WIDE), F32),
        pltpu.VMEM((2, 16, WIDE), F32),
        pltpu.VMEM((2, 16, WIDE), F32),
        pltpu.VMEM((2, 32, WIDE), F32),
        pltpu.VMEM((2, 32, WIDE), F32),
        pltpu.VMEM((2, 32, WIDE), F32),
        pltpu.VMEM((32, WIDE), F32),
        dma((2,)),
        dma((LON,)), dma((LON,)), dma((LON,)), dma((LON,)), dma((LON,)), dma((LON,)),
        dma((8,)), dma((8,)), dma((12,)), dma((12,)), dma((2,)), dma((2,)),
    ]
    return pl.pallas_call(
        kernel,
        out_shape=jax.ShapeDtypeStruct((LEV, SHARE), F32),
        in_specs=[vmem, vmem, vmem, smem, smem, hbm, hbm],
        out_specs=vmem,
        scratch_shapes=scratch,
        compiler_params=pltpu.CompilerParams(
            collective_id=0, has_side_effects=True, vmem_limit_bytes=60 * 1024 * 1024
        ),
    )(turned(wind_u), turned(wind_v), turned(vorticity), sample_level, slot_wavenumber,
      legendre_p, legendre_h)


def solution(mesh):
    placed = (
        P("lat", "lon", None),
        P("lat", "lon", None),
        P("lat", "lon", None),
        P(),
        P("lon"),
        P("lat", "lon"),
        P("lat", "lon"),
    )
    return jax.shard_map(
        body, mesh=mesh, in_specs=placed, out_specs=P(None, ("lon", "lat")), check_vma=False
    )
```

```python
import math

import jax
import jax.numpy as jnp
from jax import lax
from jax.experimental import pallas as pl
from jax.experimental.pallas import tpu as pltpu
from jax.sharding import PartitionSpec as P

NLON = 1440
NLAT = 720
MAXM = 720
LEV = 2
DAYS = 8
S = 16

LON = 32
LAT = 16
BAND = NLAT // LAT
LOCAL = NLON // LON
OWN = 23
IN_ROWS = 16
OUT_ROWS = 17
SPACE = 24
COLS = OWN * MAXM
SHARE = COLS // LAT
TALL = 264
STEP = 11

F32 = jnp.float32
BF16 = jnp.bfloat16
MESH = pl.DeviceIdType.MESH


def iota(shape, dim):
    return lax.broadcasted_iota(jnp.int32, shape, dim)


def roll64(value):
    return pltpu.roll(value, 64, 1)


def sincos(turns):
    quarter = jnp.floor(turns * (1.0 / 360.0) + 0.5)
    phi = (turns - 360.0 * quarter) * (2.0 * math.pi / NLON)
    sq = phi * phi
    s = phi * (1.0 + sq * (-1.0 / 6 + sq * (1.0 / 120 + sq * (-1.0 / 5040 + sq * (1.0 / 362880)))))
    c = 1.0 + sq * (-0.5 + sq * (1.0 / 24 + sq * (-1.0 / 720 + sq * (1.0 / 40320 - sq * (1.0 / 3628800)))))
    quad = quarter.astype(jnp.int32) & 3
    odd = (quad & 1) == 1
    cos = jnp.where(odd, s, c)
    sin = jnp.where(odd, c, s)
    cos = jnp.where((quad == 1) | (quad == 2), -cos, cos)
    sin = jnp.where(quad >= 2, -sin, sin)
    return cos, sin


def packed(source, blocks, j):
    lane = iota((32, 128), 1)
    tile = jnp.zeros((32, 128), F32)
    for t in range(blocks):
        at = t * BAND - 128 * j
        if at >= 128 or at + BAND <= 0:
            continue
        value, start = source(t)
        shift = (at - start) % 128
        value = pltpu.roll(value, shift, 1) if shift else value
        tile = jnp.where((lane >= at) & (lane < at + BAND), value, tile)
    return tile


def unpacked(tile, t):
    lane = iota((32, 128), 1)
    j, at = divmod(t * BAND, 128)
    if at == 0:
        return tile(j)
    value = pltpu.roll(tile(j), 128 - at, 1)
    if at + BAND > 128:
        value = jnp.where(lane < 128 - at, value, pltpu.roll(tile(j + 1), 128 - at, 1))
    return value


def kernel(
    u_hbm, v_hbm, z_hbm, level_ref, wave_ref, p_hbm, h_hbm, out_ref,
    u_ref, v_ref, z_ref, p_ref, h_ref, wide_p, wide_h, flux, row1, send1, recv1, wsend, wrecv,
    cos_hi, cos_lo, sin_hi, sin_lo, field, xs, coeff, row2, send2, recv2, left_p, left_h,
    toward, held, got_core, got_far, plus, minus, final, got_z,
    load_sem, wsend_sem, wrecv_sem, send1_sem, recv1_sem, send2_sem, recv2_sem,
    core_send, core_recv, x_send, x_recv, z_send, z_recv,
):
    me = lax.axis_index("lon")
    lat = lax.axis_index("lat")
    core = lax.rem(lat, 2)
    x = lax.rem(lat // 2, 4)
    half = lat // 8

    def lat_at(h, xx, cc):
        return (h * 4 + xx) * 2 + cc

    partner = lat_at(half, x, 1 - core)
    up = lat_at(half, lax.rem(x + 1, 4), core)
    down = lat_at(half, lax.rem(x + 3, 4), core)
    across = lat_at(1 - half, x, core)

    def other(k):
        return lax.rem(me + STEP * k, LON)

    load_fields = [
        pltpu.make_async_copy(src, dst, load_sem.at[2 + i])
        for i, (src, dst) in enumerate(((z_hbm, z_ref), (u_hbm, u_ref), (v_hbm, v_ref)))
    ]
    for load in load_fields:
        load.start()
    load_p = pltpu.make_async_copy(p_hbm, p_ref, load_sem.at[0])
    load_h = pltpu.make_async_copy(h_hbm, h_ref, load_sem.at[1])
    barrier = pltpu.get_barrier_semaphore()

    def greet(k, carry):
        pl.semaphore_signal(barrier, inc=1, device_id=(other(k), lat), device_id_type=MESH)
        return carry

    lax.fori_loop(1, LON, greet, 0)
    for there in (partner, up, down, across):
        pl.semaphore_signal(barrier, inc=1, device_id=(me, there), device_id_type=MESH)

    load_p.start()
    load_h.start()

    rows16 = iota((S, 128), 0)
    upper = jnp.zeros((S, 128), F32)
    for s in range(S):
        upper = jnp.where(rows16 == s, level_ref[s].astype(F32), upper)
    lower = 1.0 - upper
    upper45 = upper[None, :, :LOCAL]
    is_upper = upper45 > 0.5
    STRIP = 9

    def eddies(strip, carry):
        at = strip * STRIP

        def eddy(ref):
            value = ref[pl.ds(at, STRIP)]
            high = value * upper45
            one = jnp.sum(high, axis=1, keepdims=True) * (1.0 / DAYS)
            zero = jnp.sum(value - high, axis=1, keepdims=True) * (1.0 / DAYS)
            return value - jnp.where(is_upper, one, zero)

        row = lat * BAND + at + iota((STRIP, 1, LOCAL), 0)
        ez = eddy(z_ref) * sincos(row.astype(F32) - (0.5 * NLAT - 0.5))[0]
        fu = eddy(u_ref) * ez
        fv = eddy(v_ref) * ez
        for j in range(STRIP):
            base = pl.multiple_of((at + j) * 32, 32)
            flux[pl.ds(base, S), 0:LOCAL] = fu[j]
            flux[pl.ds(base + S, S), 0:LOCAL] = fv[j]
        return carry

    for load in load_fields:
        load.wait()
    lax.fori_loop(0, BAND // STRIP, eddies, 0)

    for j in range(IN_ROWS):
        row1[32 * j:32 * j + 32, :] = packed(lambda t: (flux[32 * t:32 * t + 32, :], 0), BAND, j)

    lane1 = iota((1, 128), 1)
    waves = jnp.full((1, 128), -1.0, F32)
    for q in range(OWN):
        waves = jnp.where(lane1 == q, wave_ref[q].astype(F32), waves)
    wsend[...] = waves
    wrecv[pl.ds(me, 1), :] = waves

    pl.semaphore_wait(barrier, LON - 1 + 4)

    def wave_copy(k, there, source):
        return pltpu.make_async_remote_copy(
            src_ref=wsend, dst_ref=wrecv.at[pl.ds(source, 1)],
            send_sem=wsend_sem.at[k], recv_sem=wrecv_sem.at[source],
            device_id=(there, lat), device_id_type=MESH,
        )

    def wave_start(k, carry):
        wave_copy(k, other(k), me).start()
        return carry

    lax.fori_loop(1, LON, wave_start, 0)

    def in_block(c):
        return pl.ds(pl.multiple_of(c * IN_ROWS, 8), IN_ROWS)

    def copy1(k, there, source):
        return pltpu.make_async_remote_copy(
            src_ref=send1.at[in_block(k)], dst_ref=recv1.at[in_block(source)],
            send_sem=send1_sem.at[k], recv_sem=recv1_sem.at[source],
            device_id=(there, lat), device_id_type=MESH,
        )

    def start1(k, carry):
        c = other(k)
        send1[in_block(k), :] = row1[pl.ds(c, IN_ROWS, stride=32), :]
        copy1(k, c, me).start()
        return carry

    lax.fori_loop(1, LON, start1, 0)
    recv1[in_block(me), :] = row1[pl.ds(me, IN_ROWS, stride=32), :]

    load_p.wait()
    load_h.wait()
    PIECE = 2048

    def widen(i, carry):
        cols = pl.ds(pl.multiple_of(i * PIECE, PIECE), PIECE)
        wide_p[:, cols] = p_ref[:, cols]
        wide_h[:, cols] = h_ref[:, cols]
        return carry

    lax.fori_loop(0, COLS // PIECE, widen, 0)
    rest = slice(COLS // PIECE * PIECE, COLS)
    wide_p[:, rest] = p_ref[:, rest]
    wide_h[:, rest] = h_ref[:, rest]

    def wave_wait(k, carry):
        wave_copy(k, other(k), other(k)).wait()
        return carry

    lax.fori_loop(1, LON, wave_wait, 0)
    lane32 = iota((32, 128), 1)

    def wave_column(q):
        return jnp.sum(jnp.where(lane32 == q, wrecv[...], 0.0), axis=1, keepdims=True)

    def split(value):
        high = value.astype(BF16)
        return high, (value - high.astype(F32)).astype(BF16)

    lon32 = ((lane32 & 63) + jnp.where(lane32 < 64, 0, LOCAL)).astype(F32)

    def tables(q, carry):
        wave = jnp.maximum(wave_column(q), 0.0)
        c, s = sincos(wave * lon32)
        rc, rs = sincos(jnp.broadcast_to(wave * (2.0 * LOCAL), (32, 128)))
        at = pl.ds(pl.multiple_of(q * 32, 32), 32)
        for j in range(8):
            lanes = slice(128 * j, 128 * (j + 1))
            ch, cl = split(c)
            sh, sl = split(s)
            cos_hi[at, lanes] = ch
            cos_lo[at, lanes] = cl
            sin_hi[at, lanes] = sh
            sin_lo[at, lanes] = sl
            c, s = c * rc - s * rs, s * rc + c * rs
        return carry

    lax.fori_loop(0, OWN, tables, 0)

    def wait1(k, carry):
        copy1(k, other(k), other(k)).wait()
        return carry

    lax.fori_loop(1, LON, wait1, 0)

    row_tile = {}

    def in_tile(j):
        if j not in row_tile:
            row_tile[j] = recv1[pl.ds(j, LON, stride=IN_ROWS), :]
        return row_tile[j]

    for t in range(BAND):
        field[pl.ds(t, LON, stride=48), :] = unpacked(in_tile, t)

    lane48 = iota((48, 128), 1)
    west = lane48 < LOCAL
    east = (lane48 >= 64) & (lane48 < 64 + LOCAL)
    for h in range(2):
        for j in range(8):
            s = 16 * h + 2 * j
            a = field[48 * s:48 * s + 48, :]
            b = field[48 * s + 48:48 * s + 96, :]
            high, low = split(jnp.where(west, a, jnp.where(east, roll64(b), 0.0)))
            lanes = slice(128 * j, 128 * (j + 1))
            xs[64 * h:64 * h + 48, lanes] = high
            xs[128 + 64 * h:176 + 64 * h, lanes] = low

    is_v = me >= S
    nt = (((1,), (1,)), ((), ()))
    def out_block(c, first, count):
        return pl.ds(pl.multiple_of(c * SPACE + first, 8), count)

    def copy2(k, there, source, first, count, sem):
        return pltpu.make_async_remote_copy(
            src_ref=send2.at[out_block(k, first, count)],
            dst_ref=recv2.at[out_block(source, first, count)],
            send_sem=send2_sem.at[sem + k], recv_sem=recv2_sem.at[sem + source],
            device_id=(there, lat), device_id_type=MESH,
        )

    parts = ((0, 12, 0, 8, 0), (12, 11, 8, OUT_ROWS - 8, LON))
    for first, count, row, rows, sem in parts:
        size = count * 32
        at = slice(first * 32, first * 32 + size)
        low_part = iota((size, 128), 1) < 64

        def transform(high_ref, low_ref):
            wide = lax.dot_general(high_ref[at, :], xs[...], nt, preferred_element_type=F32)
            thin = lax.dot_general(low_ref[at, :], xs[0:128, :], nt, preferred_element_type=F32)
            return wide[:, :128] + wide[:, 128:] + thin

        c = transform(cos_hi, cos_lo)
        s = transform(sin_hi, sin_lo)
        wave = jnp.concatenate([wave_column(q) for q in range(first, first + count)], axis=0)
        clipped = jnp.maximum(wave, 0.0)
        present = jnp.where(wave >= 0.0, 1.0 / NLON, 0.0)
        sign = 1.0 - 2.0 * (clipped - 2.0 * jnp.floor(clipped * 0.5))
        scale = clipped * (1.0 / MAXM) * present
        sin_scale = jnp.where(is_v, present, scale)
        cos_scale = jnp.where(is_v, -present, scale)
        near = jnp.where(low_part, s, roll64(c))
        far = jnp.where(low_part, roll64(s), c)
        coeff[at, :] = (near + sign * far) * jnp.where(low_part, sin_scale, cos_scale)

        for j in range(row, row + rows):
            row2[32 * j:32 * j + 32, :] = packed(
                lambda t: (coeff[32 * (t // 2):32 * (t // 2) + 32, :], 64 * (t % 2)), 2 * OWN, j
            )

        def start2(k, carry):
            o = other(k)
            send2[out_block(k, row, rows), :] = row2[pl.ds(32 * row + o, rows, stride=32), :]
            copy2(k, o, me, row, rows, sem).start()
            return carry

        lax.fori_loop(1, LON, start2, 0)
        recv2[out_block(me, row, rows), :] = row2[pl.ds(32 * row + me, rows, stride=32), :]

    for first, count, row, rows, sem in parts:

        def wait2(k, carry):
            copy2(k, other(k), other(k), row, rows, sem).wait()
            return carry

        lax.fori_loop(1, LON, wait2, 0)

    out_tiles = {}

    def out_tile(j):
        if j not in out_tiles:
            out_tiles[j] = recv2[pl.ds(j, LON, stride=SPACE), :]
        return out_tiles[j]

    for q in range(OWN):
        sin = unpacked(out_tile, 2 * q).astype(BF16)
        cos = unpacked(out_tile, 2 * q + 1).astype(BF16)
        at = slice(32 * q, 32 * q + 32)
        left_p[at, :] = jnp.concatenate([sin[:S], cos[:S]], axis=0)
        left_h[at, :] = jnp.concatenate([cos[S:], sin[S:]], axis=0)

    lane256 = iota((32, 256), 1)

    def chunk(b):
        first = SHARE * b
        tile = first // 128
        shift = first - tile * 128
        back = lax.rem(128 - shift, 128)
        inside = lane32 < 128 - shift
        turned = []
        for i in range(5):
            base = tile * 128 + 256 * i
            q = base // MAXM
            rows = pl.ds(pl.multiple_of(q * 32, 32), 64)
            cols = pl.ds(pl.multiple_of(base, 128), 256)
            r = jnp.dot(left_p[rows, 0:BAND], wide_p[:, cols], preferred_element_type=F32)
            r = r + jnp.dot(left_h[rows, 0:BAND], wide_h[:, cols], preferred_element_type=F32)
            r = jnp.where(lane256 < MAXM * (q + 1) - base, r[:32], r[32:])
            turned += [pltpu.roll(r[:, :128], back, 1), pltpu.roll(r[:, 128:], back, 1)]
        return [jnp.where(inside, turned[i], turned[i + 1]) for i in range(9)]

    def put(ref, i, b):
        pieces = chunk(b)
        for n in range(8):
            ref[i, 32 * n:32 * n + 32, :] = pieces[n]
        last = pieces[8]
        tail = last[0:8]
        for g in range(1, 4):
            tail = jnp.where(lane32[:8] < 32 * g, tail, pltpu.roll(last[8 * g:8 * g + 8], 32 * g, 1))
        ref[i, 256:264, :] = tail

    order = [(1, 2), (1, 1), (1, 3), (1, 0), (0, 2), (0, 1), (0, 3), (0, 0)]
    place = {pair: i for i, pair in enumerate(order)}

    def target(pair, cc):
        dz, dx = pair
        return lat_at(half if dz == 0 else 1 - half, lax.rem(x + dx, 4), cc)

    def send(src, dst, sends, recvs, i, there):
        return pltpu.make_async_remote_copy(
            src_ref=src, dst_ref=dst, send_sem=sends.at[i], recv_sem=recvs.at[i],
            device_id=(me, there), device_id_type=MESH,
        )

    core_copies = {}

    def give(i):
        put(toward, i, target(order[i], 1 - core))
        core_copies[i] = send(toward.at[i], got_core.at[i], core_send, core_recv, i, partner)
        core_copies[i].start()

    def keep_own(i):
        put(held, i, target(order[i], core))

    def merge(i):
        core_copies[i].wait()
        held[i] = held[i] + got_core[i]

    blocks = [
        (1, slice(0, 64), slice(64, 128)),
        (1, slice(128, 192), slice(192, TALL)),
        (0, slice(0, 128), slice(128, TALL)),
    ]
    x_copies = {}

    def x_start(i, src, dst, there):
        x_copies[i] = send(src, dst, x_send, x_recv, i, there)
        x_copies[i].start()

    def far_start(n):
        dz, a, b = blocks[n]
        i = place[(dz, 2)]
        x_start(6 * n, held.at[i, a], got_far.at[dz, a], up)
        x_start(6 * n + 1, held.at[i, b], got_far.at[dz, b], down)

    def near_start(n):
        dz, a, b = blocks[n]
        x_start(6 * n + 2, held.at[place[(dz, 1)], b], plus.at[dz, b], up)
        x_start(6 * n + 3, held.at[place[(dz, 3)], a], minus.at[dz, a], down)

    def relay(n):
        dz, a, b = blocks[n]
        i, j = place[(dz, 1)], place[(dz, 3)]
        x_copies[6 * n].wait()
        held[i, a] = held[i, a] + got_far[dz, a]
        x_start(6 * n + 4, held.at[i, a], plus.at[dz, a], up)
        x_copies[6 * n + 1].wait()
        held[j, b] = held[j, b] + got_far[dz, b]
        x_start(6 * n + 5, held.at[j, b], minus.at[dz, b], down)

    def finish(n):
        dz, a, b = blocks[n]
        own = place[(dz, 0)]
        for part, one, two in ((a, 3, 4), (b, 2, 5)):
            x_copies[6 * n + one].wait()
            x_copies[6 * n + two].wait()
            final[dz, part] = held[own, part] + plus[dz, part] + minus[dz, part]

    z_copies = []

    def z_start(n):
        part = slice(blocks[n][1].start, blocks[n][2].stop)
        copy = send(final.at[1, part], got_z.at[part], z_send, z_recv, n, across)
        copy.start()
        z_copies.append(copy)

    give(0)
    give(1)
    give(2)
    keep_own(0)
    merge(0)
    far_start(0)
    keep_own(1)
    merge(1)
    keep_own(2)
    merge(2)
    near_start(0)
    far_start(1)
    give(3)
    give(4)
    keep_own(3)
    relay(0)
    near_start(1)
    give(5)
    give(6)
    keep_own(4)
    merge(4)
    relay(1)
    far_start(2)
    give(7)
    merge(3)
    keep_own(5)
    keep_own(6)
    merge(5)
    merge(6)
    finish(0)
    z_start(0)
    near_start(2)
    finish(1)
    z_start(1)
    keep_own(7)
    merge(7)
    relay(2)
    finish(2)

    column = lat * SHARE
    slot = column // MAXM

    def power(n):
        count = SHARE - 1024 if n == 8 else 128
        if n < 8:
            value = final[0, 32 * n:32 * n + 32] + got_z[32 * n:32 * n + 32]
        else:
            tail = final[0, 256:TALL] + got_z[256:TALL]
            value = jnp.concatenate(
                [tail] + [pltpu.roll(tail, 128 - 32 * g, 1) for g in range(1, 4)], axis=0
            )
        lane = column + 128 * n + iota((1, 128), 1)
        keep = jnp.zeros((1, 128), F32)
        for d in range(3):
            q = jnp.minimum(slot + d, OWN - 1)
            wave = wave_ref[q]
            degree = lane - (slot + d) * MAXM
            good = (degree >= 0) & (degree < MAXM) & (degree >= wave) & (wave >= 0)
            keep = jnp.where(good, 1.0 / DAYS, keep)
        square = value[:S] * value[:S] + value[S:] * value[S:]
        one = jnp.sum(square * upper, axis=0, keepdims=True) * keep
        zero = jnp.sum(square * lower, axis=0, keepdims=True) * keep
        lanes = slice(128 * n, 128 * n + count)
        out_ref[0:1, lanes] = zero[:, :count]
        out_ref[1:2, lanes] = one[:, :count]

    z_copies[0].wait()
    for n in range(4):
        power(n)
    z_copies[1].wait()
    for n in range(4, 9):
        power(n)


def body(wind_u, wind_v, vorticity, sample_level, slot_wavenumber, legendre_p, legendre_h):
    def turned(field):
        return jnp.transpose(field, (0, 2, 1))

    vmem = pl.BlockSpec(memory_space=pltpu.VMEM)
    smem = pl.BlockSpec(memory_space=pltpu.SMEM)
    hbm = pl.BlockSpec(memory_space=pl.ANY)
    dma = pltpu.SemaphoreType.DMA
    block = pltpu.VMEM((BAND, S, LOCAL), F32)
    scratch = [
        block, block, block,
        pltpu.VMEM((BAND, COLS), BF16),
        pltpu.VMEM((BAND, COLS), BF16),
        pltpu.VMEM((BAND, 131 * 128), BF16),
        pltpu.VMEM((BAND, 131 * 128), BF16),
        pltpu.VMEM((BAND * 32, 128), F32),
        pltpu.VMEM((IN_ROWS * 32, 128), F32),
        pltpu.VMEM((LON * IN_ROWS, 128), F32),
        pltpu.VMEM((LON * IN_ROWS, 128), F32),
        pltpu.VMEM((1, 128), F32),
        pltpu.VMEM((LON, 128), F32),
        pltpu.VMEM((OWN * 32, 1024), BF16),
        pltpu.VMEM((OWN * 32, 1024), BF16),
        pltpu.VMEM((OWN * 32, 1024), BF16),
        pltpu.VMEM((OWN * 32, 1024), BF16),
        pltpu.VMEM((LON * 48, 128), F32),
        pltpu.VMEM((256, 1024), BF16),
        pltpu.VMEM((OWN * 32, 128), F32),
        pltpu.VMEM((OUT_ROWS * 32, 128), F32),
        pltpu.VMEM((LON * SPACE, 128), F32),
        pltpu.VMEM((LON * SPACE, 128), F32),
        pltpu.VMEM(((OWN + 1) * 32, 128), BF16),
        pltpu.VMEM(((OWN + 1) * 32, 128), BF16),
        pltpu.VMEM((8, TALL, 128), F32),
        pltpu.VMEM((8, TALL, 128), F32),
        pltpu.VMEM((8, TALL, 128), F32),
        pltpu.VMEM((2, TALL, 128), F32),
        pltpu.VMEM((2, TALL, 128), F32),
        pltpu.VMEM((2, TALL, 128), F32),
        pltpu.VMEM((2, TALL, 128), F32),
        pltpu.VMEM((TALL, 128), F32),
        dma((5,)),
        dma((LON,)), dma((LON,)), dma((LON,)), dma((LON,)), dma((2 * LON,)), dma((2 * LON,)),
        dma((8,)), dma((8,)), dma((18,)), dma((18,)), dma((2,)), dma((2,)),
    ]
    return pl.pallas_call(
        kernel,
        out_shape=jax.ShapeDtypeStruct((LEV, SHARE), F32),
        in_specs=[hbm, hbm, hbm, smem, smem, hbm, hbm],
        out_specs=vmem,
        scratch_shapes=scratch,
        compiler_params=pltpu.CompilerParams(
            collective_id=0, has_side_effects=True, vmem_limit_bytes=60 * 1024 * 1024
        ),
    )(turned(wind_u), turned(wind_v), turned(vorticity), sample_level, slot_wavenumber,
      legendre_p, legendre_h)


def solution(mesh):
    placed = (
        P("lat", "lon", None),
        P("lat", "lon", None),
        P("lat", "lon", None),
        P(),
        P("lon"),
        P("lat", "lon"),
        P("lat", "lon"),
    )
    return jax.shard_map(
        body, mesh=mesh, in_specs=placed, out_specs=P(None, ("lon", "lat")), check_vma=False
    )
```

```python
import math

import jax
import jax.numpy as jnp
from jax import lax
from jax.experimental import pallas as pl
from jax.experimental.pallas import tpu as pltpu
from jax.sharding import PartitionSpec as P

NLON = 1440
NLAT = 720
MAXM = 720
LEV = 2
DAYS = 8
S = 16

LON = 32
LAT = 16
BAND = NLAT // LAT
LOCAL = NLON // LON
OWN = 23
IN_ROWS = 16
OUT_ROWS = 17
SPACE = 24
COLS = OWN * MAXM
SHARE = COLS // LAT
TALL = 264
UNROLL = 31
STEP = 11

F32 = jnp.float32
BF16 = jnp.bfloat16
MESH = pl.DeviceIdType.MESH


def iota(shape, dim):
    return lax.broadcasted_iota(jnp.int32, shape, dim)


def roll64(value):
    return pltpu.roll(value, 64, 1)


def sincos(turns):
    quarter = jnp.floor(turns * (1.0 / 360.0) + 0.5)
    phi = (turns - 360.0 * quarter) * (2.0 * math.pi / NLON)
    sq = phi * phi
    s = phi * (1.0 + sq * (-1.0 / 6 + sq * (1.0 / 120 + sq * (-1.0 / 5040 + sq * (1.0 / 362880)))))
    c = 1.0 + sq * (-0.5 + sq * (1.0 / 24 + sq * (-1.0 / 720 + sq * (1.0 / 40320 - sq * (1.0 / 3628800)))))
    quad = quarter.astype(jnp.int32) & 3
    odd = (quad & 1) == 1
    cos = jnp.where(odd, s, c)
    sin = jnp.where(odd, c, s)
    cos = jnp.where((quad == 1) | (quad == 2), -cos, cos)
    sin = jnp.where(quad >= 2, -sin, sin)
    return cos, sin


def packed(source, blocks, j):
    lane = iota((32, 128), 1)
    tile = jnp.zeros((32, 128), F32)
    for t in range(blocks):
        at = t * BAND - 128 * j
        if at >= 128 or at + BAND <= 0:
            continue
        value, start = source(t)
        shift = (at - start) % 128
        value = pltpu.roll(value, shift, 1) if shift else value
        tile = jnp.where((lane >= at) & (lane < at + BAND), value, tile)
    return tile


def unpacked(tile, t):
    lane = iota((32, 128), 1)
    j, at = divmod(t * BAND, 128)
    if at == 0:
        return tile(j)
    value = pltpu.roll(tile(j), 128 - at, 1)
    if at + BAND > 128:
        value = jnp.where(lane < 128 - at, value, pltpu.roll(tile(j + 1), 128 - at, 1))
    return value


def kernel(
    u_hbm, v_hbm, z_hbm, level_ref, wave_ref, p_hbm, h_hbm, out_ref,
    u_ref, v_ref, z_ref, p_ref, h_ref, wide_p, wide_h, flux, row1, send1, recv1, wsend, wrecv,
    cos_hi, cos_lo, sin_hi, sin_lo, field, xs, coeff, row2, send2, recv2, left_p, left_h,
    toward, held, got_core, got_far, plus, minus, final, got_z,
    load_sem, wsend_sem, wrecv_sem, send1_sem, recv1_sem, send2_sem, recv2_sem,
    core_send, core_recv, x_send, x_recv, z_send, z_recv,
):
    me = lax.axis_index("lon")
    lat = lax.axis_index("lat")
    core = lax.rem(lat, 2)
    x = lax.rem(lat // 2, 4)
    half = lat // 8

    def lat_at(h, xx, cc):
        return (h * 4 + xx) * 2 + cc

    partner = lat_at(half, x, 1 - core)
    up = lat_at(half, lax.rem(x + 1, 4), core)
    down = lat_at(half, lax.rem(x + 3, 4), core)
    across = lat_at(1 - half, x, core)

    def other(k):
        return lax.rem(me + STEP * k, LON)

    load_fields = [
        pltpu.make_async_copy(src, dst, load_sem.at[2 + i])
        for i, (src, dst) in enumerate(((z_hbm, z_ref), (u_hbm, u_ref), (v_hbm, v_ref)))
    ]
    for load in load_fields:
        load.start()
    load_p = pltpu.make_async_copy(p_hbm, p_ref, load_sem.at[0])
    load_h = pltpu.make_async_copy(h_hbm, h_ref, load_sem.at[1])
    barrier = pltpu.get_barrier_semaphore()

    def greet(k, carry):
        pl.semaphore_signal(barrier, inc=1, device_id=(other(k), lat), device_id_type=MESH)
        return carry

    lax.fori_loop(1, LON, greet, 0, unroll=UNROLL)
    for there in (partner, up, down, across):
        pl.semaphore_signal(barrier, inc=1, device_id=(me, there), device_id_type=MESH)

    load_p.start()
    load_h.start()

    rows16 = iota((S, 128), 0)
    upper = jnp.zeros((S, 128), F32)
    for s in range(S):
        upper = jnp.where(rows16 == s, level_ref[s].astype(F32), upper)
    lower = 1.0 - upper
    upper45 = upper[None, :, :LOCAL]
    is_upper = upper45 > 0.5
    STRIP = 9

    def eddies(strip, carry):
        at = strip * STRIP

        def eddy(ref):
            value = ref[pl.ds(at, STRIP)]
            high = value * upper45
            one = jnp.sum(high, axis=1, keepdims=True) * (1.0 / DAYS)
            zero = jnp.sum(value - high, axis=1, keepdims=True) * (1.0 / DAYS)
            return value - jnp.where(is_upper, one, zero)

        row = lat * BAND + at + iota((STRIP, 1, LOCAL), 0)
        ez = eddy(z_ref) * sincos(row.astype(F32) - (0.5 * NLAT - 0.5))[0]
        fu = eddy(u_ref) * ez
        fv = eddy(v_ref) * ez
        for j in range(STRIP):
            base = pl.multiple_of((at + j) * 32, 32)
            flux[pl.ds(base, S), 0:LOCAL] = fu[j]
            flux[pl.ds(base + S, S), 0:LOCAL] = fv[j]
        return carry

    for load in load_fields:
        load.wait()
    lax.fori_loop(0, BAND // STRIP, eddies, 0)

    for j in range(IN_ROWS):
        row1[32 * j:32 * j + 32, :] = packed(lambda t: (flux[32 * t:32 * t + 32, :], 0), BAND, j)

    lane1 = iota((1, 128), 1)
    waves = jnp.full((1, 128), -1.0, F32)
    for q in range(OWN):
        waves = jnp.where(lane1 == q, wave_ref[q].astype(F32), waves)
    wsend[...] = waves
    wrecv[pl.ds(me, 1), :] = waves

    pl.semaphore_wait(barrier, LON - 1 + 4)

    def wave_copy(k, there, source):
        return pltpu.make_async_remote_copy(
            src_ref=wsend, dst_ref=wrecv.at[pl.ds(source, 1)],
            send_sem=wsend_sem.at[k], recv_sem=wrecv_sem.at[source],
            device_id=(there, lat), device_id_type=MESH,
        )

    def wave_start(k, carry):
        wave_copy(k, other(k), me).start()
        return carry

    lax.fori_loop(1, LON, wave_start, 0, unroll=UNROLL)

    def in_block(c):
        return pl.ds(pl.multiple_of(c * IN_ROWS, 8), IN_ROWS)

    def copy1(k, there, source):
        return pltpu.make_async_remote_copy(
            src_ref=send1.at[in_block(k)], dst_ref=recv1.at[in_block(source)],
            send_sem=send1_sem.at[k], recv_sem=recv1_sem.at[source],
            device_id=(there, lat), device_id_type=MESH,
        )

    def start1(k, carry):
        c = other(k)
        send1[in_block(k), :] = row1[pl.ds(c, IN_ROWS, stride=32), :]
        copy1(k, c, me).start()
        return carry

    lax.fori_loop(1, LON, start1, 0, unroll=UNROLL)
    recv1[in_block(me), :] = row1[pl.ds(me, IN_ROWS, stride=32), :]

    load_p.wait()
    load_h.wait()
    PIECE = 2048

    def widen(i, carry):
        cols = pl.ds(pl.multiple_of(i * PIECE, PIECE), PIECE)
        wide_p[:, cols] = p_ref[:, cols]
        wide_h[:, cols] = h_ref[:, cols]
        return carry

    lax.fori_loop(0, COLS // PIECE, widen, 0)
    rest = slice(COLS // PIECE * PIECE, COLS)
    wide_p[:, rest] = p_ref[:, rest]
    wide_h[:, rest] = h_ref[:, rest]

    def wave_wait(k, carry):
        wave_copy(k, other(k), other(k)).wait()
        return carry

    lax.fori_loop(1, LON, wave_wait, 0, unroll=UNROLL)
    lane32 = iota((32, 128), 1)

    def wave_column(q):
        return jnp.sum(jnp.where(lane32 == q, wrecv[...], 0.0), axis=1, keepdims=True)

    def split(value):
        high = value.astype(BF16)
        return high, (value - high.astype(F32)).astype(BF16)

    lon32 = ((lane32 & 63) + jnp.where(lane32 < 64, 0, LOCAL)).astype(F32)

    def tables(q, carry):
        wave = jnp.maximum(wave_column(q), 0.0)
        c, s = sincos(wave * lon32)
        rc, rs = sincos(jnp.broadcast_to(wave * (2.0 * LOCAL), (32, 128)))
        at = pl.ds(pl.multiple_of(q * 32, 32), 32)
        for j in range(8):
            lanes = slice(128 * j, 128 * (j + 1))
            ch, cl = split(c)
            sh, sl = split(s)
            cos_hi[at, lanes] = ch
            cos_lo[at, lanes] = cl
            sin_hi[at, lanes] = sh
            sin_lo[at, lanes] = sl
            c, s = c * rc - s * rs, s * rc + c * rs
        return carry

    lax.fori_loop(0, OWN, tables, 0)

    def wait1(k, carry):
        copy1(k, other(k), other(k)).wait()
        return carry

    lax.fori_loop(1, LON, wait1, 0, unroll=UNROLL)

    row_tile = {}

    def in_tile(j):
        if j not in row_tile:
            row_tile[j] = recv1[pl.ds(j, LON, stride=IN_ROWS), :]
        return row_tile[j]

    for t in range(BAND):
        field[pl.ds(t, LON, stride=48), :] = unpacked(in_tile, t)

    lane48 = iota((48, 128), 1)
    west = lane48 < LOCAL
    east = (lane48 >= 64) & (lane48 < 64 + LOCAL)
    for h in range(2):
        for j in range(8):
            s = 16 * h + 2 * j
            a = field[48 * s:48 * s + 48, :]
            b = field[48 * s + 48:48 * s + 96, :]
            high, low = split(jnp.where(west, a, jnp.where(east, roll64(b), 0.0)))
            lanes = slice(128 * j, 128 * (j + 1))
            xs[64 * h:64 * h + 48, lanes] = high
            xs[128 + 64 * h:176 + 64 * h, lanes] = low

    is_v = me >= S
    nt = (((1,), (1,)), ((), ()))
    def out_block(c, first, count):
        return pl.ds(pl.multiple_of(c * SPACE + first, 8), count)

    def copy2(k, there, source, first, count, sem):
        return pltpu.make_async_remote_copy(
            src_ref=send2.at[out_block(k, first, count)],
            dst_ref=recv2.at[out_block(source, first, count)],
            send_sem=send2_sem.at[sem + k], recv_sem=recv2_sem.at[sem + source],
            device_id=(there, lat), device_id_type=MESH,
        )

    parts = ((0, 12, 0, 8, 0), (12, 11, 8, OUT_ROWS - 8, LON))
    for first, count, row, rows, sem in parts:
        size = count * 32
        at = slice(first * 32, first * 32 + size)
        low_part = iota((size, 128), 1) < 64

        def transform(high_ref, low_ref):
            wide = lax.dot_general(high_ref[at, :], xs[...], nt, preferred_element_type=F32)
            thin = lax.dot_general(low_ref[at, :], xs[0:128, :], nt, preferred_element_type=F32)
            return wide[:, :128] + wide[:, 128:] + thin

        c = transform(cos_hi, cos_lo)
        s = transform(sin_hi, sin_lo)
        wave = jnp.concatenate([wave_column(q) for q in range(first, first + count)], axis=0)
        clipped = jnp.maximum(wave, 0.0)
        present = jnp.where(wave >= 0.0, 1.0 / NLON, 0.0)
        sign = 1.0 - 2.0 * (clipped - 2.0 * jnp.floor(clipped * 0.5))
        scale = clipped * (1.0 / MAXM) * present
        sin_scale = jnp.where(is_v, present, scale)
        cos_scale = jnp.where(is_v, -present, scale)
        near = jnp.where(low_part, s, roll64(c))
        far = jnp.where(low_part, roll64(s), c)
        coeff[at, :] = (near + sign * far) * jnp.where(low_part, sin_scale, cos_scale)

        for j in range(row, row + rows):
            row2[32 * j:32 * j + 32, :] = packed(
                lambda t: (coeff[32 * (t // 2):32 * (t // 2) + 32, :], 64 * (t % 2)), 2 * OWN, j
            )

        def start2(k, carry):
            o = other(k)
            send2[out_block(k, row, rows), :] = row2[pl.ds(32 * row + o, rows, stride=32), :]
            copy2(k, o, me, row, rows, sem).start()
            return carry

        lax.fori_loop(1, LON, start2, 0, unroll=UNROLL)
        recv2[out_block(me, row, rows), :] = row2[pl.ds(32 * row + me, rows, stride=32), :]

    for first, count, row, rows, sem in parts:

        def wait2(k, carry):
            copy2(k, other(k), other(k), row, rows, sem).wait()
            return carry

        lax.fori_loop(1, LON, wait2, 0, unroll=UNROLL)

    out_tiles = {}

    def out_tile(j):
        if j not in out_tiles:
            out_tiles[j] = recv2[pl.ds(j, LON, stride=SPACE), :]
        return out_tiles[j]

    for q in range(OWN):
        sin = unpacked(out_tile, 2 * q).astype(BF16)
        cos = unpacked(out_tile, 2 * q + 1).astype(BF16)
        at = slice(32 * q, 32 * q + 32)
        left_p[at, :] = jnp.concatenate([sin[:S], cos[:S]], axis=0)
        left_h[at, :] = jnp.concatenate([cos[S:], sin[S:]], axis=0)

    lane256 = iota((32, 256), 1)

    def chunk(b):
        first = SHARE * b
        tile = first // 128
        shift = first - tile * 128
        back = lax.rem(128 - shift, 128)
        inside = lane32 < 128 - shift
        turned = []
        for i in range(5):
            base = tile * 128 + 256 * i
            q = base // MAXM
            rows = pl.ds(pl.multiple_of(q * 32, 32), 64)
            cols = pl.ds(pl.multiple_of(base, 128), 256)
            r = jnp.dot(left_p[rows, 0:BAND], wide_p[:, cols], preferred_element_type=F32)
            r = r + jnp.dot(left_h[rows, 0:BAND], wide_h[:, cols], preferred_element_type=F32)
            r = jnp.where(lane256 < MAXM * (q + 1) - base, r[:32], r[32:])
            turned += [pltpu.roll(r[:, :128], back, 1), pltpu.roll(r[:, 128:], back, 1)]
        return [jnp.where(inside, turned[i], turned[i + 1]) for i in range(9)]

    def put(ref, i, b):
        pieces = chunk(b)
        for n in range(8):
            ref[i, 32 * n:32 * n + 32, :] = pieces[n]
        last = pieces[8]
        tail = last[0:8]
        for g in range(1, 4):
            tail = jnp.where(lane32[:8] < 32 * g, tail, pltpu.roll(last[8 * g:8 * g + 8], 32 * g, 1))
        ref[i, 256:264, :] = tail

    order = [(1, 2), (1, 1), (1, 3), (1, 0), (0, 2), (0, 1), (0, 3), (0, 0)]
    place = {pair: i for i, pair in enumerate(order)}

    def target(pair, cc):
        dz, dx = pair
        return lat_at(half if dz == 0 else 1 - half, lax.rem(x + dx, 4), cc)

    def send(src, dst, sends, recvs, i, there):
        return pltpu.make_async_remote_copy(
            src_ref=src, dst_ref=dst, send_sem=sends.at[i], recv_sem=recvs.at[i],
            device_id=(me, there), device_id_type=MESH,
        )

    core_copies = {}

    def give(i):
        put(toward, i, target(order[i], 1 - core))
        core_copies[i] = send(toward.at[i], got_core.at[i], core_send, core_recv, i, partner)
        core_copies[i].start()

    def keep_own(i):
        put(held, i, target(order[i], core))

    def merge(i):
        core_copies[i].wait()
        held[i] = held[i] + got_core[i]

    blocks = [
        (1, slice(0, 64), slice(64, 128)),
        (1, slice(128, 192), slice(192, TALL)),
        (0, slice(0, 128), slice(128, TALL)),
    ]
    x_copies = {}

    def x_start(i, src, dst, there):
        x_copies[i] = send(src, dst, x_send, x_recv, i, there)
        x_copies[i].start()

    def far_start(n):
        dz, a, b = blocks[n]
        i = place[(dz, 2)]
        x_start(6 * n, held.at[i, a], got_far.at[dz, a], up)
        x_start(6 * n + 1, held.at[i, b], got_far.at[dz, b], down)

    def near_start(n):
        dz, a, b = blocks[n]
        x_start(6 * n + 2, held.at[place[(dz, 1)], b], plus.at[dz, b], up)
        x_start(6 * n + 3, held.at[place[(dz, 3)], a], minus.at[dz, a], down)

    def relay(n):
        dz, a, b = blocks[n]
        i, j = place[(dz, 1)], place[(dz, 3)]
        x_copies[6 * n].wait()
        held[i, a] = held[i, a] + got_far[dz, a]
        x_start(6 * n + 4, held.at[i, a], plus.at[dz, a], up)
        x_copies[6 * n + 1].wait()
        held[j, b] = held[j, b] + got_far[dz, b]
        x_start(6 * n + 5, held.at[j, b], minus.at[dz, b], down)

    def finish(n):
        dz, a, b = blocks[n]
        own = place[(dz, 0)]
        for part, one, two in ((a, 3, 4), (b, 2, 5)):
            x_copies[6 * n + one].wait()
            x_copies[6 * n + two].wait()
            final[dz, part] = held[own, part] + plus[dz, part] + minus[dz, part]

    z_copies = []

    def z_start(n):
        part = slice(blocks[n][1].start, blocks[n][2].stop)
        copy = send(final.at[1, part], got_z.at[part], z_send, z_recv, n, across)
        copy.start()
        z_copies.append(copy)

    for i in range(4):
        give(i)
    keep_own(0)
    give(4)
    keep_own(1)
    give(5)
    keep_own(2)
    give(6)
    give(7)
    merge(0)
    far_start(0)
    merge(1)
    merge(2)
    near_start(0)
    far_start(1)
    keep_own(3)
    merge(3)
    keep_own(4)
    merge(4)
    keep_own(5)
    merge(5)
    keep_own(6)
    merge(6)
    relay(0)
    near_start(1)
    relay(1)
    far_start(2)
    near_start(2)
    keep_own(7)
    merge(7)
    finish(0)
    z_start(0)
    finish(1)
    z_start(1)
    relay(2)
    finish(2)

    column = lat * SHARE
    slot = column // MAXM

    def power(n):
        count = SHARE - 1024 if n == 8 else 128
        if n < 8:
            value = final[0, 32 * n:32 * n + 32] + got_z[32 * n:32 * n + 32]
        else:
            tail = final[0, 256:TALL] + got_z[256:TALL]
            value = jnp.concatenate(
                [tail] + [pltpu.roll(tail, 128 - 32 * g, 1) for g in range(1, 4)], axis=0
            )
        lane = column + 128 * n + iota((1, 128), 1)
        keep = jnp.zeros((1, 128), F32)
        for d in range(3):
            q = jnp.minimum(slot + d, OWN - 1)
            wave = wave_ref[q]
            degree = lane - (slot + d) * MAXM
            good = (degree >= 0) & (degree < MAXM) & (degree >= wave) & (wave >= 0)
            keep = jnp.where(good, 1.0 / DAYS, keep)
        square = value[:S] * value[:S] + value[S:] * value[S:]
        one = jnp.sum(square * upper, axis=0, keepdims=True) * keep
        zero = jnp.sum(square * lower, axis=0, keepdims=True) * keep
        lanes = slice(128 * n, 128 * n + count)
        out_ref[0:1, lanes] = zero[:, :count]
        out_ref[1:2, lanes] = one[:, :count]

    z_copies[0].wait()
    for n in range(4):
        power(n)
    z_copies[1].wait()
    for n in range(4, 9):
        power(n)


def body(wind_u, wind_v, vorticity, sample_level, slot_wavenumber, legendre_p, legendre_h):
    def turned(field):
        return jnp.transpose(field, (0, 2, 1))

    vmem = pl.BlockSpec(memory_space=pltpu.VMEM)
    smem = pl.BlockSpec(memory_space=pltpu.SMEM)
    hbm = pl.BlockSpec(memory_space=pl.ANY)
    dma = pltpu.SemaphoreType.DMA
    block = pltpu.VMEM((BAND, S, LOCAL), F32)
    scratch = [
        block, block, block,
        pltpu.VMEM((BAND, COLS), BF16),
        pltpu.VMEM((BAND, COLS), BF16),
        pltpu.VMEM((BAND, 131 * 128), BF16),
        pltpu.VMEM((BAND, 131 * 128), BF16),
        pltpu.VMEM((BAND * 32, 128), F32),
        pltpu.VMEM((IN_ROWS * 32, 128), F32),
        pltpu.VMEM((LON * IN_ROWS, 128), F32),
        pltpu.VMEM((LON * IN_ROWS, 128), F32),
        pltpu.VMEM((1, 128), F32),
        pltpu.VMEM((LON, 128), F32),
        pltpu.VMEM((OWN * 32, 1024), BF16),
        pltpu.VMEM((OWN * 32, 1024), BF16),
        pltpu.VMEM((OWN * 32, 1024), BF16),
        pltpu.VMEM((OWN * 32, 1024), BF16),
        pltpu.VMEM((LON * 48, 128), F32),
        pltpu.VMEM((256, 1024), BF16),
        pltpu.VMEM((OWN * 32, 128), F32),
        pltpu.VMEM((OUT_ROWS * 32, 128), F32),
        pltpu.VMEM((LON * SPACE, 128), F32),
        pltpu.VMEM((LON * SPACE, 128), F32),
        pltpu.VMEM(((OWN + 1) * 32, 128), BF16),
        pltpu.VMEM(((OWN + 1) * 32, 128), BF16),
        pltpu.VMEM((8, TALL, 128), F32),
        pltpu.VMEM((8, TALL, 128), F32),
        pltpu.VMEM((8, TALL, 128), F32),
        pltpu.VMEM((2, TALL, 128), F32),
        pltpu.VMEM((2, TALL, 128), F32),
        pltpu.VMEM((2, TALL, 128), F32),
        pltpu.VMEM((2, TALL, 128), F32),
        pltpu.VMEM((TALL, 128), F32),
        dma((5,)),
        dma((LON,)), dma((LON,)), dma((LON,)), dma((LON,)), dma((2 * LON,)), dma((2 * LON,)),
        dma((8,)), dma((8,)), dma((18,)), dma((18,)), dma((2,)), dma((2,)),
    ]
    return pl.pallas_call(
        kernel,
        out_shape=jax.ShapeDtypeStruct((LEV, SHARE), F32),
        in_specs=[hbm, hbm, hbm, smem, smem, hbm, hbm],
        out_specs=vmem,
        scratch_shapes=scratch,
        compiler_params=pltpu.CompilerParams(
            collective_id=0, has_side_effects=True, vmem_limit_bytes=60 * 1024 * 1024
        ),
    )(turned(wind_u), turned(wind_v), turned(vorticity), sample_level, slot_wavenumber,
      legendre_p, legendre_h)


def solution(mesh):
    placed = (
        P("lat", "lon", None),
        P("lat", "lon", None),
        P("lat", "lon", None),
        P(),
        P("lon"),
        P("lat", "lon"),
        P("lat", "lon"),
    )
    return jax.shard_map(
        body, mesh=mesh, in_specs=placed, out_specs=P(None, ("lon", "lat")), check_vma=False
    )
```

```python
import math

import jax
import jax.numpy as jnp
from jax import lax
from jax.experimental import pallas as pl
from jax.experimental.pallas import tpu as pltpu
from jax.sharding import PartitionSpec as P

NLON = 1440
NLAT = 720
MAXM = 720
LEV = 2
DAYS = 8
S = 16

LON = 32
LAT = 16
BAND = NLAT // LAT
LOCAL = NLON // LON
OWN = 23
IN_ROWS = 16
OUT_ROWS = 17
SPACE = 24
COLS = OWN * MAXM
SHARE = COLS // LAT
TALL = 264
UNROLL = 31
STEP = 11

F32 = jnp.float32
BF16 = jnp.bfloat16
MESH = pl.DeviceIdType.MESH


def iota(shape, dim):
    return lax.broadcasted_iota(jnp.int32, shape, dim)


def roll64(value):
    return pltpu.roll(value, 64, 1)


def sincos(turns):
    quarter = jnp.floor(turns * (1.0 / 360.0) + 0.5)
    phi = (turns - 360.0 * quarter) * (2.0 * math.pi / NLON)
    sq = phi * phi
    s = phi * (1.0 + sq * (-1.0 / 6 + sq * (1.0 / 120 + sq * (-1.0 / 5040 + sq * (1.0 / 362880)))))
    c = 1.0 + sq * (-0.5 + sq * (1.0 / 24 + sq * (-1.0 / 720 + sq * (1.0 / 40320 - sq * (1.0 / 3628800)))))
    quad = quarter.astype(jnp.int32) & 3
    odd = (quad & 1) == 1
    cos = jnp.where(odd, s, c)
    sin = jnp.where(odd, c, s)
    cos = jnp.where((quad == 1) | (quad == 2), -cos, cos)
    sin = jnp.where(quad >= 2, -sin, sin)
    return cos, sin


def packed(source, blocks, j):
    lane = iota((32, 128), 1)
    tile = jnp.zeros((32, 128), F32)
    for t in range(blocks):
        at = t * BAND - 128 * j
        if at >= 128 or at + BAND <= 0:
            continue
        value, start = source(t)
        shift = (at - start) % 128
        value = pltpu.roll(value, shift, 1) if shift else value
        tile = jnp.where((lane >= at) & (lane < at + BAND), value, tile)
    return tile


def unpacked(tile, t):
    lane = iota((32, 128), 1)
    j, at = divmod(t * BAND, 128)
    if at == 0:
        return tile(j)
    value = pltpu.roll(tile(j), 128 - at, 1)
    if at + BAND > 128:
        value = jnp.where(lane < 128 - at, value, pltpu.roll(tile(j + 1), 128 - at, 1))
    return value


def kernel(
    u_hbm, v_hbm, z_hbm, level_ref, wave_ref, p_hbm, h_hbm, out_ref,
    u_ref, v_ref, z_ref, p_ref, h_ref, wide_p, wide_h, flux, row1, send1, recv1, wsend, wrecv,
    cos_hi, cos_lo, sin_hi, sin_lo, field, xs, coeff, row2, send2, recv2, left_p, left_h,
    toward, held, got_core, got_far, plus, minus, final, got_z,
    load_sem, wsend_sem, wrecv_sem, send1_sem, recv1_sem, send2_sem, recv2_sem,
    core_send, core_recv, x_send, x_recv, z_send, z_recv,
):
    me = lax.axis_index("lon")
    lat = lax.axis_index("lat")
    core = lax.rem(lat, 2)
    x = lax.rem(lat // 2, 4)
    half = lat // 8

    def lat_at(h, xx, cc):
        return (h * 4 + xx) * 2 + cc

    partner = lat_at(half, x, 1 - core)
    up = lat_at(half, lax.rem(x + 1, 4), core)
    down = lat_at(half, lax.rem(x + 3, 4), core)
    across = lat_at(1 - half, x, core)

    def other(k):
        return lax.rem(me + STEP * k, LON)

    load_fields = [
        pltpu.make_async_copy(src, dst, load_sem.at[2 + i])
        for i, (src, dst) in enumerate(((z_hbm, z_ref), (u_hbm, u_ref), (v_hbm, v_ref)))
    ]
    for load in load_fields:
        load.start()
    load_p = pltpu.make_async_copy(p_hbm, p_ref, load_sem.at[0])
    load_h = pltpu.make_async_copy(h_hbm, h_ref, load_sem.at[1])
    barrier = pltpu.get_barrier_semaphore()

    def greet(k, carry):
        pl.semaphore_signal(barrier, inc=1, device_id=(other(k), lat), device_id_type=MESH)
        return carry

    lax.fori_loop(1, LON, greet, 0, unroll=UNROLL)
    for there in (partner, up, down, across):
        pl.semaphore_signal(barrier, inc=1, device_id=(me, there), device_id_type=MESH)

    load_p.start()
    load_h.start()

    rows16 = iota((S, 128), 0)
    upper = jnp.zeros((S, 128), F32)
    for s in range(S):
        upper = jnp.where(rows16 == s, level_ref[s].astype(F32), upper)
    lower = 1.0 - upper
    upper45 = upper[None, :, :LOCAL]
    is_upper = upper45 > 0.5
    STRIP = 9

    def eddies(strip, carry):
        at = strip * STRIP

        def eddy(ref):
            value = ref[pl.ds(at, STRIP)]
            high = value * upper45
            one = jnp.sum(high, axis=1, keepdims=True) * (1.0 / DAYS)
            zero = jnp.sum(value - high, axis=1, keepdims=True) * (1.0 / DAYS)
            return value - jnp.where(is_upper, one, zero)

        row = lat * BAND + at + iota((STRIP, 1, LOCAL), 0)
        ez = eddy(z_ref) * sincos(row.astype(F32) - (0.5 * NLAT - 0.5))[0]
        fu = eddy(u_ref) * ez
        fv = eddy(v_ref) * ez
        for j in range(STRIP):
            base = pl.multiple_of((at + j) * 32, 32)
            flux[pl.ds(base, S), 0:LOCAL] = fu[j]
            flux[pl.ds(base + S, S), 0:LOCAL] = fv[j]
        return carry

    for load in load_fields:
        load.wait()
    lax.fori_loop(0, BAND // STRIP, eddies, 0)

    for j in range(IN_ROWS):
        row1[32 * j:32 * j + 32, :] = packed(lambda t: (flux[32 * t:32 * t + 32, :], 0), BAND, j)

    lane1 = iota((1, 128), 1)
    waves = jnp.full((1, 128), -1.0, F32)
    for q in range(OWN):
        waves = jnp.where(lane1 == q, wave_ref[q].astype(F32), waves)
    wsend[...] = waves
    wrecv[pl.ds(me, 1), :] = waves

    pl.semaphore_wait(barrier, LON - 1 + 4)

    def wave_copy(k, there, source):
        return pltpu.make_async_remote_copy(
            src_ref=wsend, dst_ref=wrecv.at[pl.ds(source, 1)],
            send_sem=wsend_sem.at[k], recv_sem=wrecv_sem.at[source],
            device_id=(there, lat), device_id_type=MESH,
        )

    def wave_start(k, carry):
        wave_copy(k, other(k), me).start()
        return carry

    lax.fori_loop(1, LON, wave_start, 0, unroll=UNROLL)

    def in_block(c):
        return pl.ds(pl.multiple_of(c * IN_ROWS, 8), IN_ROWS)

    def copy1(k, there, source):
        return pltpu.make_async_remote_copy(
            src_ref=send1.at[in_block(k)], dst_ref=recv1.at[in_block(source)],
            send_sem=send1_sem.at[k], recv_sem=recv1_sem.at[source],
            device_id=(there, lat), device_id_type=MESH,
        )

    def start1(k, carry):
        c = other(k)
        send1[in_block(k), :] = row1[pl.ds(c, IN_ROWS, stride=32), :]
        copy1(k, c, me).start()
        return carry

    lax.fori_loop(1, LON, start1, 0, unroll=UNROLL)
    recv1[in_block(me), :] = row1[pl.ds(me, IN_ROWS, stride=32), :]

    load_p.wait()
    load_h.wait()
    PIECE = 2048

    def widen(i, carry):
        cols = pl.ds(pl.multiple_of(i * PIECE, PIECE), PIECE)
        wide_p[:, cols] = p_ref[:, cols]
        wide_h[:, cols] = h_ref[:, cols]
        return carry

    lax.fori_loop(0, COLS // PIECE, widen, 0)
    rest = slice(COLS // PIECE * PIECE, COLS)
    wide_p[:, rest] = p_ref[:, rest]
    wide_h[:, rest] = h_ref[:, rest]

    def wave_wait(k, carry):
        wave_copy(k, other(k), other(k)).wait()
        return carry

    lax.fori_loop(1, LON, wave_wait, 0, unroll=UNROLL)
    lane32 = iota((32, 128), 1)

    def wave_column(q):
        return jnp.sum(jnp.where(lane32 == q, wrecv[...], 0.0), axis=1, keepdims=True)

    def split(value):
        high = value.astype(BF16)
        return high, (value - high.astype(F32)).astype(BF16)

    lon32 = ((lane32 & 63) + jnp.where(lane32 < 64, 0, LOCAL)).astype(F32)

    def tables(q, carry):
        wave = jnp.maximum(wave_column(q), 0.0)
        c, s = sincos(wave * lon32)
        rc, rs = sincos(jnp.broadcast_to(wave * (2.0 * LOCAL), (32, 128)))
        at = pl.ds(pl.multiple_of(q * 32, 32), 32)
        for j in range(8):
            lanes = slice(128 * j, 128 * (j + 1))
            ch, cl = split(c)
            sh, sl = split(s)
            cos_hi[at, lanes] = ch
            cos_lo[at, lanes] = cl
            sin_hi[at, lanes] = sh
            sin_lo[at, lanes] = sl
            c, s = c * rc - s * rs, s * rc + c * rs
        return carry

    lax.fori_loop(0, OWN, tables, 0)

    def wait1(k, carry):
        copy1(k, other(k), other(k)).wait()
        return carry

    lax.fori_loop(1, LON, wait1, 0, unroll=UNROLL)

    row_tile = {}

    def in_tile(j):
        if j not in row_tile:
            row_tile[j] = recv1[pl.ds(j, LON, stride=IN_ROWS), :]
        return row_tile[j]

    for t in range(BAND):
        field[pl.ds(t, LON, stride=48), :] = unpacked(in_tile, t)

    lane48 = iota((48, 128), 1)
    west = lane48 < LOCAL
    east = (lane48 >= 64) & (lane48 < 64 + LOCAL)
    for h in range(2):
        for j in range(8):
            s = 16 * h + 2 * j
            a = field[48 * s:48 * s + 48, :]
            b = field[48 * s + 48:48 * s + 96, :]
            high, low = split(jnp.where(west, a, jnp.where(east, roll64(b), 0.0)))
            lanes = slice(128 * j, 128 * (j + 1))
            xs[64 * h:64 * h + 48, lanes] = high
            xs[128 + 64 * h:176 + 64 * h, lanes] = low

    is_v = me >= S
    nt = (((1,), (1,)), ((), ()))
    def out_block(c, first, count):
        return pl.ds(pl.multiple_of(c * SPACE + first, 8), count)

    def copy2(k, there, source, first, count, sem):
        return pltpu.make_async_remote_copy(
            src_ref=send2.at[out_block(k, first, count)],
            dst_ref=recv2.at[out_block(source, first, count)],
            send_sem=send2_sem.at[sem + k], recv_sem=recv2_sem.at[sem + source],
            device_id=(there, lat), device_id_type=MESH,
        )

    parts = ((0, 12, 0, 8, 0), (12, 11, 8, OUT_ROWS - 8, LON))
    for first, count, row, rows, sem in parts:
        size = count * 32
        at = slice(first * 32, first * 32 + size)
        low_part = iota((size, 128), 1) < 64

        def transform(high_ref, low_ref):
            wide = lax.dot_general(high_ref[at, :], xs[...], nt, preferred_element_type=F32)
            thin = lax.dot_general(low_ref[at, :], xs[0:128, :], nt, preferred_element_type=F32)
            return wide[:, :128] + wide[:, 128:] + thin

        c = transform(cos_hi, cos_lo)
        s = transform(sin_hi, sin_lo)
        wave = jnp.concatenate([wave_column(q) for q in range(first, first + count)], axis=0)
        clipped = jnp.maximum(wave, 0.0)
        present = jnp.where(wave >= 0.0, 1.0 / NLON, 0.0)
        sign = 1.0 - 2.0 * (clipped - 2.0 * jnp.floor(clipped * 0.5))
        scale = clipped * (1.0 / MAXM) * present
        sin_scale = jnp.where(is_v, present, scale)
        cos_scale = jnp.where(is_v, -present, scale)
        near = jnp.where(low_part, s, roll64(c))
        far = jnp.where(low_part, roll64(s), c)
        coeff[at, :] = (near + sign * far) * jnp.where(low_part, sin_scale, cos_scale)

        for j in range(row, row + rows):
            row2[32 * j:32 * j + 32, :] = packed(
                lambda t: (coeff[32 * (t // 2):32 * (t // 2) + 32, :], 64 * (t % 2)), 2 * OWN, j
            )

        def start2(k, carry):
            o = other(k)
            send2[out_block(k, row, rows), :] = row2[pl.ds(32 * row + o, rows, stride=32), :]
            copy2(k, o, me, row, rows, sem).start()
            return carry

        lax.fori_loop(1, LON, start2, 0, unroll=UNROLL)
        recv2[out_block(me, row, rows), :] = row2[pl.ds(32 * row + me, rows, stride=32), :]

    for first, count, row, rows, sem in parts:

        def wait2(k, carry):
            copy2(k, other(k), other(k), row, rows, sem).wait()
            return carry

        lax.fori_loop(1, LON, wait2, 0, unroll=UNROLL)

    out_tiles = {}

    def out_tile(j):
        if j not in out_tiles:
            out_tiles[j] = recv2[pl.ds(j, LON, stride=SPACE), :]
        return out_tiles[j]

    for q in range(OWN):
        sin = unpacked(out_tile, 2 * q).astype(BF16)
        cos = unpacked(out_tile, 2 * q + 1).astype(BF16)
        at = slice(32 * q, 32 * q + 32)
        left_p[at, :] = jnp.concatenate([sin[:S], cos[:S]], axis=0)
        left_h[at, :] = jnp.concatenate([cos[S:], sin[S:]], axis=0)

    lane256 = iota((32, 256), 1)

    def chunk(b):
        first = SHARE * b
        tile = first // 128
        shift = first - tile * 128
        back = lax.rem(128 - shift, 128)
        inside = lane32 < 128 - shift
        turned = []
        for i in range(5):
            base = tile * 128 + 256 * i
            q = base // MAXM
            rows = pl.ds(pl.multiple_of(q * 32, 32), 64)
            cols = pl.ds(pl.multiple_of(base, 128), 256)
            r = jnp.dot(left_p[rows, 0:BAND], wide_p[:, cols], preferred_element_type=F32)
            r = r + jnp.dot(left_h[rows, 0:BAND], wide_h[:, cols], preferred_element_type=F32)
            r = jnp.where(lane256 < MAXM * (q + 1) - base, r[:32], r[32:])
            turned += [pltpu.roll(r[:, :128], back, 1), pltpu.roll(r[:, 128:], back, 1)]
        return [jnp.where(inside, turned[i], turned[i + 1]) for i in range(9)]

    def put(ref, i, b):
        pieces = chunk(b)
        for n in range(8):
            ref[i, 32 * n:32 * n + 32, :] = pieces[n]
        last = pieces[8]
        tail = last[0:8]
        for g in range(1, 4):
            tail = jnp.where(lane32[:8] < 32 * g, tail, pltpu.roll(last[8 * g:8 * g + 8], 32 * g, 1))
        ref[i, 256:264, :] = tail

    order = [(1, 2), (1, 1), (1, 3), (1, 0), (0, 2), (0, 1), (0, 3), (0, 0)]
    place = {pair: i for i, pair in enumerate(order)}

    def target(pair, cc):
        dz, dx = pair
        return lat_at(half if dz == 0 else 1 - half, lax.rem(x + dx, 4), cc)

    def send(src, dst, sends, recvs, i, there):
        return pltpu.make_async_remote_copy(
            src_ref=src, dst_ref=dst, send_sem=sends.at[i], recv_sem=recvs.at[i],
            device_id=(me, there), device_id_type=MESH,
        )

    core_copies = {}

    def give(i):
        put(toward, i, target(order[i], 1 - core))
        core_copies[i] = send(toward.at[i], got_core.at[i], core_send, core_recv, i, partner)
        core_copies[i].start()

    def keep_own(i):
        put(held, i, target(order[i], core))

    def merge(i):
        core_copies[i].wait()
        held[i] = held[i] + got_core[i]

    blocks = [
        (1, slice(0, 64), slice(64, 128)),
        (1, slice(128, 192), slice(192, TALL)),
        (0, slice(0, 128), slice(128, TALL)),
    ]
    x_copies = {}

    def x_start(i, src, dst, there):
        x_copies[i] = send(src, dst, x_send, x_recv, i, there)
        x_copies[i].start()

    def far_start(n):
        dz, a, b = blocks[n]
        i = place[(dz, 2)]
        x_start(6 * n, held.at[i, a], got_far.at[dz, a], up)
        x_start(6 * n + 1, held.at[i, b], got_far.at[dz, b], down)

    def near_start(n):
        dz, a, b = blocks[n]
        x_start(6 * n + 2, held.at[place[(dz, 1)], b], plus.at[dz, b], up)
        x_start(6 * n + 3, held.at[place[(dz, 3)], a], minus.at[dz, a], down)

    def relay(n):
        dz, a, b = blocks[n]
        i, j = place[(dz, 1)], place[(dz, 3)]
        x_copies[6 * n].wait()
        held[i, a] = held[i, a] + got_far[dz, a]
        x_start(6 * n + 4, held.at[i, a], plus.at[dz, a], up)
        x_copies[6 * n + 1].wait()
        held[j, b] = held[j, b] + got_far[dz, b]
        x_start(6 * n + 5, held.at[j, b], minus.at[dz, b], down)

    def finish(n):
        dz, a, b = blocks[n]
        own = place[(dz, 0)]
        for part, one, two in ((a, 3, 4), (b, 2, 5)):
            x_copies[6 * n + one].wait()
            x_copies[6 * n + two].wait()
            final[dz, part] = held[own, part] + plus[dz, part] + minus[dz, part]

    z_copies = []

    def z_start(n):
        part = slice(blocks[n][1].start, blocks[n][2].stop)
        copy = send(final.at[1, part], got_z.at[part], z_send, z_recv, n, across)
        copy.start()
        z_copies.append(copy)

    for i in range(4):
        give(i)
    for i in range(3):
        keep_own(i)
    merge(0)
    far_start(0)
    merge(1)
    merge(2)
    near_start(0)
    far_start(1)
    for i in range(4, 8):
        give(i)
    keep_own(3)
    merge(3)
    keep_own(4)
    relay(0)
    near_start(1)
    merge(4)
    keep_own(5)
    merge(5)
    keep_own(6)
    merge(6)
    relay(1)
    far_start(2)
    near_start(2)
    keep_own(7)
    merge(7)
    finish(0)
    z_start(0)
    finish(1)
    z_start(1)
    relay(2)
    finish(2)

    column = lat * SHARE
    slot = column // MAXM

    def power(n):
        count = SHARE - 1024 if n == 8 else 128
        if n < 8:
            value = final[0, 32 * n:32 * n + 32] + got_z[32 * n:32 * n + 32]
        else:
            tail = final[0, 256:TALL] + got_z[256:TALL]
            value = jnp.concatenate(
                [tail] + [pltpu.roll(tail, 128 - 32 * g, 1) for g in range(1, 4)], axis=0
            )
        lane = column + 128 * n + iota((1, 128), 1)
        keep = jnp.zeros((1, 128), F32)
        for d in range(3):
            q = jnp.minimum(slot + d, OWN - 1)
            wave = wave_ref[q]
            degree = lane - (slot + d) * MAXM
            good = (degree >= 0) & (degree < MAXM) & (degree >= wave) & (wave >= 0)
            keep = jnp.where(good, 1.0 / DAYS, keep)
        square = value[:S] * value[:S] + value[S:] * value[S:]
        one = jnp.sum(square * upper, axis=0, keepdims=True) * keep
        zero = jnp.sum(square * lower, axis=0, keepdims=True) * keep
        lanes = slice(128 * n, 128 * n + count)
        out_ref[0:1, lanes] = zero[:, :count]
        out_ref[1:2, lanes] = one[:, :count]

    z_copies[0].wait()
    for n in range(4):
        power(n)
    z_copies[1].wait()
    for n in range(4, 9):
        power(n)


def body(wind_u, wind_v, vorticity, sample_level, slot_wavenumber, legendre_p, legendre_h):
    def turned(field):
        return jnp.transpose(field, (0, 2, 1))

    vmem = pl.BlockSpec(memory_space=pltpu.VMEM)
    smem = pl.BlockSpec(memory_space=pltpu.SMEM)
    hbm = pl.BlockSpec(memory_space=pl.ANY)
    dma = pltpu.SemaphoreType.DMA
    block = pltpu.VMEM((BAND, S, LOCAL), F32)
    scratch = [
        block, block, block,
        pltpu.VMEM((BAND, COLS), BF16),
        pltpu.VMEM((BAND, COLS), BF16),
        pltpu.VMEM((BAND, 131 * 128), BF16),
        pltpu.VMEM((BAND, 131 * 128), BF16),
        pltpu.VMEM((BAND * 32, 128), F32),
        pltpu.VMEM((IN_ROWS * 32, 128), F32),
        pltpu.VMEM((LON * IN_ROWS, 128), F32),
        pltpu.VMEM((LON * IN_ROWS, 128), F32),
        pltpu.VMEM((1, 128), F32),
        pltpu.VMEM((LON, 128), F32),
        pltpu.VMEM((OWN * 32, 1024), BF16),
        pltpu.VMEM((OWN * 32, 1024), BF16),
        pltpu.VMEM((OWN * 32, 1024), BF16),
        pltpu.VMEM((OWN * 32, 1024), BF16),
        pltpu.VMEM((LON * 48, 128), F32),
        pltpu.VMEM((256, 1024), BF16),
        pltpu.VMEM((OWN * 32, 128), F32),
        pltpu.VMEM((OUT_ROWS * 32, 128), F32),
        pltpu.VMEM((LON * SPACE, 128), F32),
        pltpu.VMEM((LON * SPACE, 128), F32),
        pltpu.VMEM(((OWN + 1) * 32, 128), BF16),
        pltpu.VMEM(((OWN + 1) * 32, 128), BF16),
        pltpu.VMEM((8, TALL, 128), F32),
        pltpu.VMEM((8, TALL, 128), F32),
        pltpu.VMEM((8, TALL, 128), F32),
        pltpu.VMEM((2, TALL, 128), F32),
        pltpu.VMEM((2, TALL, 128), F32),
        pltpu.VMEM((2, TALL, 128), F32),
        pltpu.VMEM((2, TALL, 128), F32),
        pltpu.VMEM((TALL, 128), F32),
        dma((5,)),
        dma((LON,)), dma((LON,)), dma((LON,)), dma((LON,)), dma((2 * LON,)), dma((2 * LON,)),
        dma((8,)), dma((8,)), dma((18,)), dma((18,)), dma((2,)), dma((2,)),
    ]
    return pl.pallas_call(
        kernel,
        out_shape=jax.ShapeDtypeStruct((LEV, SHARE), F32),
        in_specs=[hbm, hbm, hbm, smem, smem, hbm, hbm],
        out_specs=vmem,
        scratch_shapes=scratch,
        compiler_params=pltpu.CompilerParams(
            collective_id=0, has_side_effects=True, vmem_limit_bytes=60 * 1024 * 1024
        ),
    )(turned(wind_u), turned(wind_v), turned(vorticity), sample_level, slot_wavenumber,
      legendre_p, legendre_h)


def solution(mesh):
    placed = (
        P("lat", "lon", None),
        P("lat", "lon", None),
        P("lat", "lon", None),
        P(),
        P("lon"),
        P("lat", "lon"),
        P("lat", "lon"),
    )
    return jax.shard_map(
        body, mesh=mesh, in_specs=placed, out_specs=P(None, ("lon", "lat")), check_vma=False
    )
```
